512 devices in a mesh: tm: 64 (over y, z), chan: 8 (over x, core).
Axes of the slice: x: 4, y: 8, z: 8, core: 2. Of those that a mesh axis runs over, the one named last changes fastest.
Arguments:
- frames: bfloat16 [512, 16, 16, 256], P('tm'), may hold values from -6 to 6
- in_weight: bfloat16 [3, 3, 256, 1024], P(None, None, None, 'chan'), may hold values from -0.125 to 0.125
- decay_codes: int32 [1024], P('chan'), may hold values from 1 to 20
- out_weight: bfloat16 [3, 3, 1024, 256], P(None, None, 'chan'), may hold values from -0.00390625 to 0.00390625
- skip_gain: float32 [256], replicated, may hold values from 0.5 to 1.5
Outputs:
- mixed: bfloat16 [512, 16, 16, 256], P('tm', 'chan')
The draws below stay inside these ranges and needn't reach their ends.
Inputs may be any that keep to these rules, and one draw needn't show every extreme that they name: `decay_codes`: a code k gives the channel the decay 1 - k / 4096.
All inputs are finite; a program needn't handle non-finite values.
Results may differ from the reference program's by a relative error of at most 0.0037.
Values sent between devices are 32-bit elements; how exact they have to be, the bound alone decides.
No kernel may reach another device: no remote copies, remote signals or barrier semaphores. Data moves between devices by JAX's collectives and lax.ppermute only.
A program may use at most 64 MiB of HBM per device.

```python
import jax
import jax.numpy as jnp
from jax import lax

CIN = 256
P_SIZE = 1024
H = 16
W = 16
TT = 512


def with_ends(entries, rng, smallest, top_value):
    dims = entries.shape
    place = [jax.random.randint(jax.random.fold_in(rng, axis), (), 0, dims[axis]) for axis in range(len(dims))]
    entries = entries.at[tuple(place)].set(smallest)
    longest = dims.index(max(dims))
    place[longest] = (place[longest] + 1) % dims[longest]
    return entries.at[tuple(place)].set(top_value)


def shard_levels(own_key, dims, pieces, low, high):
    factor_of = 1.0
    for position, shards_of in pieces:
        draws = jax.random.uniform(jax.random.fold_in(jax.random.fold_in(own_key, 6), position), (shards_of,), jnp.float32, low / len(pieces), high / len(pieces))
        factor_of = factor_of * jnp.repeat(jnp.exp(draws), dims[position] // shards_of).reshape((-1,) + (1,) * (len(dims) - 1 - position))
    return factor_of


def normal_values(rng, extent, scale, limit, shards=(), dtype=jnp.bfloat16):
    drawn = scale * jax.random.normal(rng, extent, jnp.float32)
    if shards:
        drawn = drawn * shard_levels(rng, extent, shards, -0.22, 0.18)
    return jnp.clip(drawn, -limit, limit).astype(dtype)


def setup_inputs(seed: int = 0) -> dict:
    arg_keys = jax.random.split(jax.random.key(seed), 6)
    return {
        "frames": normal_values(arg_keys[0], (TT, H, W, CIN), 1.0, 6.0, ((0, 64),)),
        "in_weight": normal_values(arg_keys[1], (3, 3, CIN, P_SIZE), (9 * CIN) ** -0.5, 0.125, ((3, 8),)),
        "decay_codes": with_ends(jax.random.randint(arg_keys[2], (P_SIZE,), 1, 21), jax.random.fold_in(arg_keys[2], 1), 1, 20).astype(jnp.int32),
        "out_weight": normal_values(arg_keys[3], (3, 3, P_SIZE, CIN), (9 * P_SIZE * 256) ** -0.5, 0.00390625, ((2, 8),)),
        "skip_gain": jnp.clip(jax.random.uniform(arg_keys[4], (CIN,), jnp.float32, 0.5, 1.5), 0.5, 1.5),
    }


def convolve(inputs, kernel):
    return lax.conv_general_dilated(inputs, kernel, (1, 1), "SAME", dimension_numbers=("NHWC", "HWIO", "NHWC"), preferred_element_type=jnp.float32)


def reference(frames, in_weight, decay_codes, out_weight, skip_gain):
    drive_term = convolve(frames, in_weight)
    decay_rate = 1.0 - decay_codes.astype(jnp.float32) / 4096.0

    def advance_step(carry_state, drive_frame):
        carry_state = decay_rate * carry_state + drive_frame
        return carry_state, carry_state

    final_state, states = lax.scan(advance_step, jnp.zeros(drive_term.shape[1:], jnp.float32), drive_term)
    state_b = states.astype(jnp.bfloat16)
    combined = convolve(state_b, out_weight) + skip_gain * frames.astype(jnp.float32)
    return jax.nn.gelu(combined, approximate=False).astype(jnp.bfloat16)
```

```python
import jax
import jax.numpy as jnp
from jax import lax
from jax.experimental import pallas as pl
from jax.experimental.pallas import tpu as pltpu
from jax.sharding import Mesh
from jax.sharding import PartitionSpec as P

VMEM = pl.BlockSpec(memory_space=pltpu.VMEM)
SMEM = pl.BlockSpec(memory_space=pltpu.SMEM)
FRAMES, ROWS, COLS, CIN, PD = 8, 16, 16, 256, 128
PIX = ROWS * COLS
F32, BF16 = jnp.float32, jnp.bfloat16


def decay_of(codes):
    return 1.0 - codes.astype(F32) / 4096.0


def pow8(value):
    value = value * value
    value = value * value
    return value * value


def shifted_sum(left, centre, right):
    count = left.shape[0]
    column = lax.broadcasted_iota(jnp.int32, left.shape, 0) % COLS
    from_left = jnp.where(column == 0, 0.0, pltpu.roll(left, 1, 0))
    from_right = jnp.where(column == COLS - 1, 0.0, pltpu.roll(right, count - 1, 0))
    return from_left + centre + from_right


def drive_kernel(x_ref, w_ref, codes_ref, states_ref, end_ref, xpad, wcat):
    xpad[:, 0] = jnp.zeros((FRAMES, COLS, CIN), BF16)
    xpad[:, ROWS + 1] = jnp.zeros((FRAMES, COLS, CIN), BF16)
    xpad[:, 1 : ROWS + 1] = x_ref[...]
    for di in range(3):
        for dj in range(3):
            wcat[di, :, dj * PD : (dj + 1) * PD] = w_ref[di, dj]
    decay = decay_of(codes_ref[...])
    running = jnp.zeros((PIX, PD), F32)
    group = 2
    for first in range(0, FRAMES, group):
        total = jnp.zeros((group * PIX, 3 * PD), F32)
        for di in range(3):
            rows = xpad[first : first + group, di : di + ROWS].reshape(group * PIX, CIN)
            total = total + jnp.dot(rows, wcat[di], preferred_element_type=F32)
        drive = shifted_sum(total[:, :PD], total[:, PD : 2 * PD], total[:, 2 * PD :])
        for k in range(group):
            running = decay * running + drive[k * PIX : (k + 1) * PIX]
            states_ref[(first + k) * PIX : (first + k + 1) * PIX] = running
    states_ref[FRAMES * PIX :] = jnp.broadcast_to(decay, (8, PD))
    end_ref[...] = running.reshape(8, PIX // 8, PD)


def total_kernel(ends_ref, codes_ref, out_ref):
    a8 = pow8(decay_of(codes_ref[...]))
    total = ends_ref[0]
    for z in range(1, 8):
        total = a8 * total + ends_ref[z]
    for y in range(8):
        out_ref[y] = total


def carry_kernel(place_ref, ends_ref, totals_ref, codes_ref, out_ref):
    a8 = pow8(decay_of(codes_ref[...]))
    a64 = pow8(a8)
    own = place_ref[0]
    carry = jnp.zeros((PIX // 8, PD), F32)
    for y in range(8):
        carry = jnp.where(y < own, a64 * carry + totals_ref[y], carry)
    for z in range(8):
        out_ref[2 * z] = carry
        out_ref[2 * z + 1] = carry
        carry = a8 * carry + ends_ref[z]


def readout_kernel(place_ref, own_ref, other_ref, carry_ref, w_ref, out_ref, spad):
    core = place_ref[1]
    zeros = jnp.zeros((FRAMES, COLS, 2 * PD), BF16)
    spad[:, 0] = zeros
    spad[:, ROWS + 1] = zeros
    for side, (ref, which) in enumerate(((own_ref, core), (other_ref, 1 - core))):
        decay = ref[FRAMES * PIX : FRAMES * PIX + 1]
        carry = carry_ref[:, pl.ds(which, 1)].reshape(PIX, PD)
        for j in range(FRAMES):
            carry = decay * carry
            state = ref[j * PIX : (j + 1) * PIX] + carry
            spad[j, 1 : ROWS + 1, :, side * PD : (side + 1) * PD] = state.astype(BF16).reshape(ROWS, COLS, PD)
    taps = []
    rows = [
        jnp.concatenate(
            [
                spad[:, pl.ds(4 * x + 2 * core + di, 2)].reshape(FRAMES * 2 * COLS, 2 * PD)
                for x in range(4)
            ],
            axis=0,
        )
        for di in range(3)
    ]
    for dj in range(3):
        total = jnp.dot(rows[0], w_ref[0, dj], preferred_element_type=F32)
        for di in range(1, 3):
            total = total + jnp.dot(rows[di], w_ref[di, dj], preferred_element_type=F32)
        taps.append(total)
    out_ref[...] = shifted_sum(*taps)


def widen_kernel(w_ref, out_ref):
    out_ref[...] = w_ref[...].astype(F32)


def merge_kernel(own_ref, other_ref, out_ref):
    out_ref[:, :, :PD] = own_ref[...]
    out_ref[:, :, PD:] = other_ref[...].astype(BF16)


def call(kernel, out, args, scratch=(), smem=0, flops=0, moved=1 << 20):
    return pl.pallas_call(
        kernel,
        out_shape=out,
        in_specs=[SMEM] * smem + [VMEM] * (len(args) - smem),
        out_specs=jax.tree.map(lambda _: VMEM, out),
        scratch_shapes=list(scratch),
        compiler_params=pltpu.CompilerParams(vmem_limit_bytes=40 << 20),
        cost_estimate=pl.CostEstimate(flops=flops, bytes_accessed=moved, transcendentals=0),
    )(*args)


def shape(*dims, dtype=F32):
    return jax.ShapeDtypeStruct(dims, dtype)


def per_device(frames, in_weight, decay_codes, out_weight, skip_gain):
    codes = decay_codes.reshape(1, PD)
    place = jnp.stack([lax.axis_index("y"), lax.axis_index("c")]).astype(jnp.int32)
    flops = 2 * FRAMES * PIX * 9 * CIN * PD
    states, end = call(
        drive_kernel,
        (shape(FRAMES * PIX + 8, PD), shape(8, PIX // 8, PD)),
        (frames, in_weight, codes),
        scratch=(
            pltpu.VMEM((FRAMES, ROWS + 2, COLS, CIN), BF16),
            pltpu.VMEM((3, CIN, 3 * PD), BF16),
        ),
        flops=flops,
        moved=3 << 20,
    )
    swap = [(0, 1), (1, 0)]
    ends = lax.all_to_all(end, "z", 0, 0, tiled=True)
    weight_other = lax.ppermute(call(widen_kernel, shape(3, 3, PD, CIN), (out_weight,)), "c", swap)
    states_other = lax.ppermute(states, "c", swap)
    weights = call(merge_kernel, shape(3, 3, 2 * PD, CIN, dtype=BF16), (out_weight, weight_other))
    total = call(total_kernel, shape(8, PIX // 8, PD), (ends, codes))
    totals = lax.all_to_all(total, "y", 0, 0, tiled=True)
    carries = call(carry_kernel, shape(16, PIX // 8, PD), (place, ends, totals, codes), smem=1)
    carry = lax.all_to_all(carries, ("z", "c"), 0, 0, tiled=True).reshape(8, 2, PIX // 8, PD)
    partial_value = call(
        readout_kernel,
        shape(4 * FRAMES * 2 * COLS, CIN),
        (place, states, states_other, carry, weights),
        scratch=(pltpu.VMEM((FRAMES, ROWS + 2, COLS, 2 * PD), BF16),),
        smem=1,
        flops=flops,
        moved=4 << 20,
    ).reshape(4, FRAMES, 2, COLS, CIN)
    arrived = lax.all_to_all(partial_value, "x", 0, 0, tiled=True)
    start_row = 2 * (2 * lax.axis_index("x") + lax.axis_index("c"))
    own_frames = lax.dynamic_slice_in_dim(frames, start_row, 2, 1).astype(F32)
    return jax.nn.gelu(arrived.sum(axis=0) + skip_gain * own_frames, approximate=False).astype(BF16)


def solution(mesh):
    finer = Mesh(mesh.devices.reshape(8, 8, 4, 2), ("y", "z", "x", "c"))
    chan = ("x", "c")
    placed = (
        P(("y", "z"), None, None, None),
        P(None, None, None, chan),
        P(chan),
        P(None, None, chan, None),
        P(),
    )
    return jax.shard_map(
        per_device,
        mesh=finer,
        in_specs=placed,
        out_specs=P(("y", "z"), chan, None, None),
        check_vma=False,
    )
```

```python
import jax
import jax.numpy as jnp
from jax import lax
from jax.experimental import pallas as pl
from jax.experimental.pallas import tpu as pltpu
from jax.sharding import Mesh
from jax.sharding import PartitionSpec as P

VMEM = pl.BlockSpec(memory_space=pltpu.VMEM)
SMEM = pl.BlockSpec(memory_space=pltpu.SMEM)
FRAMES, ROWS, COLS, CIN, PD = 8, 16, 16, 256, 128
PIX = ROWS * COLS
DECAY_AT = FRAMES * PIX
WEIGHT_AT = DECAY_AT + 8
SHARED = WEIGHT_AT + 18 * PD
F32, BF16 = jnp.float32, jnp.bfloat16


def decay_of(codes):
    return 1.0 - codes.astype(F32) / 4096.0


def pow8(value):
    value = value * value
    value = value * value
    return value * value


def shifted_sum(left, centre, right):
    count = left.shape[0]
    column = lax.broadcasted_iota(jnp.int32, left.shape, 0) % COLS
    from_left = jnp.where(column == 0, 0.0, pltpu.roll(left, 1, 0))
    from_right = jnp.where(column == COLS - 1, 0.0, pltpu.roll(right, count - 1, 0))
    return from_left + centre + from_right


def drive_kernel(place_ref, x_ref, w_ref, codes_ref, wout_ref, gain_ref, states_ref, end_ref, skip_ref, xpad, wcat):
    xpad[:, 0] = jnp.zeros((FRAMES, COLS, CIN), BF16)
    xpad[:, ROWS + 1] = jnp.zeros((FRAMES, COLS, CIN), BF16)
    xpad[:, 1 : ROWS + 1] = x_ref[...]
    for di in range(3):
        for dj in range(3):
            wcat[di, :, dj * PD : (dj + 1) * PD] = w_ref[di, dj]
    decay = decay_of(codes_ref[...])
    running = jnp.zeros((PIX, PD), F32)
    group = 2
    for first in range(0, FRAMES, group):
        total = jnp.zeros((group * PIX, 3 * PD), F32)
        for di in range(3):
            rows = xpad[first : first + group, di : di + ROWS].reshape(group * PIX, CIN)
            total = total + jnp.dot(rows, wcat[di], preferred_element_type=F32)
        drive = shifted_sum(total[:, :PD], total[:, PD : 2 * PD], total[:, 2 * PD :])
        for k in range(group):
            running = decay * running + drive[k * PIX : (k + 1) * PIX]
            states_ref[(first + k) * PIX : (first + k + 1) * PIX] = running
    end_ref[...] = running.reshape(8, PIX // 8, PD)
    states_ref[DECAY_AT:WEIGHT_AT] = jnp.broadcast_to(decay, (8, PD))
    for tap in range(9):
        for half in range(2):
            at = WEIGHT_AT + (2 * tap + half) * PD
            states_ref[at : at + PD] = wout_ref[tap // 3, tap % 3, :, half * PD : (half + 1) * PD].astype(F32)
    own = x_ref[:, pl.ds(place_ref[2], 2)].reshape(FRAMES * 2 * COLS, CIN)
    skip_ref[...] = own.astype(F32) * gain_ref[...]


def total_kernel(ends_ref, codes_ref, wout_ref, other_ref, out_ref, w_ref):
    a8 = pow8(decay_of(codes_ref[...]))
    total = ends_ref[0]
    for z in range(1, 8):
        total = a8 * total + ends_ref[z]
    for y in range(8):
        out_ref[y] = total
    w_ref[:, :, :PD] = wout_ref[...]
    for tap in range(9):
        for half in range(2):
            at = WEIGHT_AT + (2 * tap + half) * PD
            w_ref[tap // 3, tap % 3, PD:, half * PD : (half + 1) * PD] = other_ref[at : at + PD].astype(BF16)


def mix_kernel(parts_ref, skip_ref, out_ref):
    value = parts_ref[0] + parts_ref[1] + parts_ref[2] + parts_ref[3] + skip_ref[...]
    half = 0.5 * value
    mixed = half + half * lax.erf(value * (0.5**0.5))
    out_ref[...] = mixed.astype(BF16)


def carry_kernel(place_ref, ends_ref, totals_ref, codes_ref, out_ref):
    a8 = pow8(decay_of(codes_ref[...]))
    a64 = pow8(a8)
    own = place_ref[0]
    carry = jnp.zeros((PIX // 8, PD), F32)
    for y in range(8):
        carry = jnp.where(y < own, a64 * carry + totals_ref[y], carry)
    for z in range(8):
        out_ref[2 * z] = carry
        out_ref[2 * z + 1] = carry
        carry = a8 * carry + ends_ref[z]


def readout_kernel(place_ref, own_ref, other_ref, carry_ref, w_ref, out_ref, spad):
    core = place_ref[1]
    zeros = jnp.zeros((FRAMES, COLS, 2 * PD), BF16)
    spad[:, 0] = zeros
    spad[:, ROWS + 1] = zeros
    for side, (ref, which) in enumerate(((own_ref, core), (other_ref, 1 - core))):
        decay = ref[DECAY_AT : DECAY_AT + 1]
        carry = carry_ref[:, pl.ds(which, 1)].reshape(PIX, PD)
        for j in range(FRAMES):
            carry = decay * carry
            state = ref[j * PIX : (j + 1) * PIX] + carry
            spad[j, 1 : ROWS + 1, :, side * PD : (side + 1) * PD] = state.astype(BF16).reshape(ROWS, COLS, PD)
    taps = []
    rows = [
        jnp.concatenate(
            [
                spad[:, pl.ds(4 * x + 2 * core + di, 2)].reshape(FRAMES * 2 * COLS, 2 * PD)
                for x in range(4)
            ],
            axis=0,
        )
        for di in range(3)
    ]
    for dj in range(3):
        total = jnp.dot(rows[0], w_ref[0, dj], preferred_element_type=F32)
        for di in range(1, 3):
            total = total + jnp.dot(rows[di], w_ref[di, dj], preferred_element_type=F32)
        taps.append(total)
    out_ref[...] = shifted_sum(*taps)


def call(kernel, out, args, scratch=(), smem=0, flops=0, moved=1 << 20):
    return pl.pallas_call(
        kernel,
        out_shape=out,
        in_specs=[SMEM] * smem + [VMEM] * (len(args) - smem),
        out_specs=jax.tree.map(lambda _: VMEM, out),
        scratch_shapes=list(scratch),
        compiler_params=pltpu.CompilerParams(vmem_limit_bytes=24 << 20),
        cost_estimate=pl.CostEstimate(flops=flops, bytes_accessed=moved, transcendentals=0),
    )(*args)


def shape(*dims, dtype=F32):
    return jax.ShapeDtypeStruct(dims, dtype)


def per_device(frames, in_weight, decay_codes, out_weight, skip_gain):
    codes = decay_codes.reshape(1, PD)
    y, x, core = lax.axis_index("y"), lax.axis_index("x"), lax.axis_index("c")
    place = jnp.stack([y, core, 4 * x + 2 * core]).astype(jnp.int32)
    flops = 2 * FRAMES * PIX * 9 * CIN * PD
    slices = shape(8, PIX // 8, PD)
    owned = FRAMES * 2 * COLS
    states, end, skip = call(
        drive_kernel,
        (shape(SHARED, PD), slices, shape(owned, CIN)),
        (place, frames, in_weight, codes, out_weight, skip_gain.reshape(1, CIN)),
        scratch=(
            pltpu.VMEM((FRAMES, ROWS + 2, COLS, CIN), BF16),
            pltpu.VMEM((3, CIN, 3 * PD), BF16),
        ),
        smem=1,
        flops=flops,
        moved=3 << 20,
    )
    ends = lax.all_to_all(end, "z", 0, 0, tiled=True)
    states_other = lax.ppermute(states, "c", [(0, 1), (1, 0)])
    total, weights = call(
        total_kernel,
        (slices, shape(3, 3, 2 * PD, CIN, dtype=BF16)),
        (ends, codes, out_weight, states_other),
    )
    totals = lax.all_to_all(total, "y", 0, 0, tiled=True)
    carries = call(carry_kernel, shape(16, PIX // 8, PD), (place, ends, totals, codes), smem=1)
    carry = lax.all_to_all(carries, ("z", "c"), 0, 0, tiled=True).reshape(8, 2, PIX // 8, PD)
    partial_value = call(
        readout_kernel,
        shape(4 * owned, CIN),
        (place, states, states_other, carry, weights),
        scratch=(pltpu.VMEM((FRAMES, ROWS + 2, COLS, 2 * PD), BF16),),
        smem=1,
        flops=flops,
        moved=4 << 20,
    ).reshape(4, owned, CIN)
    arrived = lax.all_to_all(partial_value, "x", 0, 0, tiled=True)
    mixed = call(mix_kernel, shape(owned, CIN, dtype=BF16), (arrived, skip))
    return mixed.reshape(FRAMES, 2, COLS, CIN)


def solution(mesh):
    finer = Mesh(mesh.devices.reshape(8, 8, 4, 2), ("y", "z", "x", "c"))
    chan = ("x", "c")
    placed = (
        P(("y", "z"), None, None, None),
        P(None, None, None, chan),
        P(chan),
        P(None, None, chan, None),
        P(),
    )
    return jax.shard_map(
        per_device,
        mesh=finer,
        in_specs=placed,
        out_specs=P(("y", "z"), chan, None, None),
        check_vma=False,
    )
```

```python
import jax
import jax.numpy as jnp
from jax import lax
from jax.experimental import pallas as pl
from jax.experimental.pallas import tpu as pltpu
from jax.sharding import Mesh
from jax.sharding import PartitionSpec as P

FRAMES, ROWS, COLS, CIN, PD = 8, 16, 16, 256, 128
PIX = ROWS * COLS
DECAY_AT = FRAMES * PIX
WEIGHT_AT = DECAY_AT + 8
SHARED = WEIGHT_AT + 18 * PD
F32, BF16 = jnp.float32, jnp.bfloat16


def decay_of(codes):
    return 1.0 - codes.astype(F32) / 4096.0


def pow8(value):
    value = value * value
    value = value * value
    return value * value


def shifted_sum(left, centre, right):
    count = left.shape[0]
    column = lax.broadcasted_iota(jnp.int32, left.shape, 0) % COLS
    from_left = jnp.where(column == 0, 0.0, pltpu.roll(left, 1, 0))
    from_right = jnp.where(column == COLS - 1, 0.0, pltpu.roll(right, count - 1, 0))
    return from_left + centre + from_right


def drive_kernel(place_ref, x_hbm, w_hbm, codes_hbm, wout_hbm, gain_hbm,
                 shared_hbm, end_ref, skip_ref, decay_ref,
                 xpad, wcat, wout, codes, gain, shared, frame_sem, tap_sem, small_sem, out_sem):
    taps = [(di, dj) for di in range(3) for dj in range(3)]
    copies = [
        pltpu.make_async_copy(w_hbm.at[di, dj], wcat.at[di, :, pl.ds(dj * PD, PD)], tap_sem.at[3 * di + dj])
        for di, dj in taps
    ]
    frames = [
        pltpu.make_async_copy(x_hbm.at[j], xpad.at[j, pl.ds(1, ROWS)], frame_sem.at[j]) for j in range(FRAMES)
    ]
    small = [
        pltpu.make_async_copy(src, dst, small_sem.at[i])
        for i, (src, dst) in enumerate(((codes_hbm, codes), (wout_hbm, wout), (gain_hbm, gain)))
    ]
    group = 2
    edges = [*range(0, DECAY_AT, group * PIX), DECAY_AT, SHARED]
    sends = [
        pltpu.make_async_copy(shared.at[pl.ds(at, to - at)], shared_hbm.at[pl.ds(at, to - at)], out_sem.at[i])
        for i, (at, to) in enumerate(zip(edges[:-1], edges[1:], strict=True))
    ]
    for copy in [small[0], *frames[:2], *copies, small[1], *frames[2:], small[2]]:
        copy.start()
    xpad[:, 0] = jnp.zeros((FRAMES, COLS, CIN), BF16)
    xpad[:, ROWS + 1] = jnp.zeros((FRAMES, COLS, CIN), BF16)
    small[0].wait()
    decay = decay_of(codes[...])
    decay_ref[...] = decay
    shared[DECAY_AT:WEIGHT_AT] = jnp.broadcast_to(decay, (8, PD))
    for copy in copies:
        copy.wait()
    running = jnp.zeros((PIX, PD), F32)
    for first in range(0, FRAMES, group):
        total = jnp.zeros((group * PIX, 3 * PD), F32)
        for copy in frames[first : first + group]:
            copy.wait()
        for di in range(3):
            rows = xpad[first : first + group, di : di + ROWS].reshape(group * PIX, CIN)
            total = total + jnp.dot(rows, wcat[di], preferred_element_type=F32)
        drive = shifted_sum(total[:, :PD], total[:, PD : 2 * PD], total[:, 2 * PD :])
        for k in range(group):
            running = decay * running + drive[k * PIX : (k + 1) * PIX]
            shared[(first + k) * PIX : (first + k + 1) * PIX] = running
        sends[first // group].start()
        if first == 0:
            small[1].wait()
            for tap in range(9):
                for half in range(2):
                    at = WEIGHT_AT + (2 * tap + half) * PD
                    shared[at : at + PD] = wout[tap // 3, tap % 3, :, half * PD : (half + 1) * PD].astype(F32)
            sends[-1].start()
    end_ref[...] = running.reshape(8, PIX // 8, PD)
    small[2].wait()
    own = xpad[:, pl.ds(place_ref[2] + 1, 2)].reshape(FRAMES * 2 * COLS, CIN)
    skip_ref[...] = own.astype(F32) * gain[...]
    for copy in sends:
        copy.wait()


def total_kernel(ends_ref, decay_ref, out_ref):
    a8 = pow8(decay_ref[...])
    total = ends_ref[0]
    for z in range(1, 8):
        total = a8 * total + ends_ref[z]
    for y in range(8):
        out_ref[y] = total


def mix_kernel(parts_ref, skip_ref, out_ref):
    value = parts_ref[0] + parts_ref[1] + parts_ref[2] + parts_ref[3] + skip_ref[...]
    half = 0.5 * value
    mixed = half + half * lax.erf(value * (0.5**0.5))
    out_ref[...] = mixed.astype(BF16)


def carry_kernel(place_ref, ends_ref, totals_ref, decay_ref, wout_ref, other_ref, out_ref, w_ref):
    a8 = pow8(decay_ref[...])
    a64 = pow8(a8)
    own = place_ref[0]
    carry = jnp.zeros((PIX // 8, PD), F32)
    for y in range(8):
        carry = jnp.where(y < own, a64 * carry + totals_ref[y], carry)
    for z in range(8):
        out_ref[z] = carry
        carry = a8 * carry + ends_ref[z]
    w_ref[:, :, :PD] = wout_ref[...]
    for tap in range(9):
        for half in range(2):
            at = WEIGHT_AT + (2 * tap + half) * PD
            w_ref[tap // 3, tap % 3, PD:, half * PD : (half + 1) * PD] = other_ref[at : at + PD].astype(BF16)


def readout_kernel(place_ref, own_ref, other_ref, decay_ref, carry_ref, carry_other_ref, w_ref, out_ref, spad):
    core = place_ref[1]
    zeros = jnp.zeros((FRAMES, COLS, 2 * PD), BF16)
    spad[:, 0] = zeros
    spad[:, ROWS + 1] = zeros
    sides = (
        (own_ref, carry_ref, decay_ref[...]),
        (other_ref, carry_other_ref, other_ref[DECAY_AT : DECAY_AT + 1]),
    )
    for side, (ref, carried, decay) in enumerate(sides):
        carry = carried[...].reshape(PIX, PD)
        for j in range(FRAMES):
            carry = decay * carry
            state = ref[j * PIX : (j + 1) * PIX] + carry
            spad[j, 1 : ROWS + 1, :, side * PD : (side + 1) * PD] = state.astype(BF16).reshape(ROWS, COLS, PD)
    taps = []
    rows = [
        jnp.concatenate(
            [
                spad[:, pl.ds(4 * x + 2 * core + di, 2)].reshape(FRAMES * 2 * COLS, 2 * PD)
                for x in range(4)
            ],
            axis=0,
        )
        for di in range(3)
    ]
    for dj in range(3):
        total = jnp.dot(rows[0], w_ref[0, dj], preferred_element_type=F32)
        for di in range(1, 3):
            total = total + jnp.dot(rows[di], w_ref[di, dj], preferred_element_type=F32)
        taps.append(total)
    out_ref[...] = shifted_sum(*taps)


def call(kernel, out, args, spaces=None, scratch=(), flops=0, moved=1 << 20, limit=24, outs=None):
    return pl.pallas_call(
        kernel,
        out_shape=out,
        in_specs=[pl.BlockSpec(memory_space=space) for space in spaces or [pltpu.VMEM] * len(args)],
        out_specs=outs or jax.tree.map(lambda _: pl.BlockSpec(memory_space=pltpu.VMEM), out),
        scratch_shapes=list(scratch),
        compiler_params=pltpu.CompilerParams(vmem_limit_bytes=limit << 20),
        cost_estimate=pl.CostEstimate(flops=flops, bytes_accessed=moved, transcendentals=0),
    )(*args)


def shape(*dims, dtype=F32):
    return jax.ShapeDtypeStruct(dims, dtype)


def per_device(frames, in_weight, decay_codes, out_weight, skip_gain):
    codes = decay_codes.reshape(1, PD)
    y, x, core = lax.axis_index("y"), lax.axis_index("x"), lax.axis_index("c")
    place = jnp.stack([y, core, 4 * x + 2 * core]).astype(jnp.int32)
    flops = 2 * FRAMES * PIX * 9 * CIN * PD
    slices = shape(8, PIX // 8, PD)
    owned = FRAMES * 2 * COLS
    shared, end, skip, decay = call(
        drive_kernel,
        (shape(SHARED, PD), slices, shape(owned, CIN), shape(1, PD)),
        (place, frames, in_weight, codes, out_weight, skip_gain.reshape(1, CIN)),
        spaces=[pltpu.SMEM] + [pltpu.HBM] * 5,
        scratch=(
            pltpu.VMEM((FRAMES, ROWS + 2, COLS, CIN), BF16),
            pltpu.VMEM((3, CIN, 3 * PD), BF16),
            pltpu.VMEM((3, 3, PD, CIN), BF16),
            pltpu.VMEM((1, PD), jnp.int32),
            pltpu.VMEM((1, CIN), F32),
            pltpu.VMEM((SHARED, PD), F32),
            pltpu.SemaphoreType.DMA((FRAMES,)),
            pltpu.SemaphoreType.DMA((9,)),
            pltpu.SemaphoreType.DMA((3,)),
            pltpu.SemaphoreType.DMA((5,)),
        ),
        flops=flops,
        moved=3 << 20,
        limit=59,
        outs=tuple(pl.BlockSpec(memory_space=space) for space in (pltpu.HBM,) + (pltpu.VMEM,) * 3),
    )
    swap = [(0, 1), (1, 0)]
    ends = lax.all_to_all(end, "z", 0, 0, tiled=True)
    other = lax.ppermute(shared, "c", swap)
    total = call(total_kernel, slices, (ends, decay))
    totals = lax.all_to_all(total, "y", 0, 0, tiled=True)
    carries, weights = call(
        carry_kernel,
        (slices, shape(3, 3, 2 * PD, CIN, dtype=BF16)),
        (place, ends, totals, decay, out_weight, other),
        spaces=[pltpu.SMEM] + [pltpu.VMEM] * 5,
    )
    carry = lax.all_to_all(carries, "z", 0, 0, tiled=True)
    carry_other = lax.ppermute(carry, "c", swap)
    partial_value = call(
        readout_kernel,
        shape(4 * owned, CIN),
        (place, shared, other, decay, carry, carry_other, weights),
        spaces=[pltpu.SMEM] + [pltpu.VMEM] * 6,
        scratch=(pltpu.VMEM((FRAMES, ROWS + 2, COLS, 2 * PD), BF16),),
        flops=flops,
        moved=4 << 20,
    ).reshape(4, owned, CIN)
    arrived = lax.all_to_all(partial_value, "x", 0, 0, tiled=True)
    mixed = call(mix_kernel, shape(owned, CIN, dtype=BF16), (arrived, skip))
    return mixed.reshape(FRAMES, 2, COLS, CIN)


def solution(mesh):
    finer = Mesh(mesh.devices.reshape(8, 8, 4, 2), ("y", "z", "x", "c"))
    chan = ("x", "c")
    placed = (
        P(("y", "z"), None, None, None),
        P(None, None, None, chan),
        P(chan),
        P(None, None, chan, None),
        P(),
    )
    return jax.shard_map(
        per_device,
        mesh=finer,
        in_specs=placed,
        out_specs=P(("y", "z"), chan, None, None),
        check_vma=False,
    )
```

```python
import functools


import jax
import jax.numpy as jnp
from jax import lax
from jax.experimental import pallas as pl
from jax.experimental.pallas import tpu as pltpu
from jax.sharding import Mesh
from jax.sharding import PartitionSpec as P

FRAMES, ROWS, COLS, CIN, PD = 8, 16, 16, 256, 128
PIX = ROWS * COLS
DECAY_AT = FRAMES * PIX
WEIGHT_AT = DECAY_AT + 8
SHARED = WEIGHT_AT + 18 * PD
F32, BF16 = jnp.float32, jnp.bfloat16


def decay_of(codes):
    return 1.0 - codes.astype(F32) / 4096.0


def pow8(value):
    value = value * value
    value = value * value
    return value * value


def shifted_sum(left, centre, right):
    count = left.shape[0]
    column = lax.broadcasted_iota(jnp.int32, left.shape, 0) % COLS
    from_left = jnp.where(column == 0, 0.0, pltpu.roll(left, 1, 0))
    from_right = jnp.where(column == COLS - 1, 0.0, pltpu.roll(right, count - 1, 0))
    return from_left + centre + from_right


def drive_kernel(x_hbm, w_hbm, codes_hbm, wout_hbm, shared_hbm, end_ref,
                 xpad, wcat, wout, codes, shared, frame_sem, tap_sem, small_sem, out_sem):
    taps = [(di, dj) for di in range(3) for dj in range(3)]
    copies = [
        pltpu.make_async_copy(w_hbm.at[di, dj], wcat.at[di, :, pl.ds(dj * PD, PD)], tap_sem.at[3 * di + dj])
        for di, dj in taps
    ]
    frames = [
        pltpu.make_async_copy(x_hbm.at[j], xpad.at[j, pl.ds(1, ROWS)], frame_sem.at[j]) for j in range(FRAMES)
    ]
    small = [
        pltpu.make_async_copy(src, dst, small_sem.at[i])
        for i, (src, dst) in enumerate(((codes_hbm, codes), (wout_hbm, wout)))
    ]
    group = 2
    edges = [*range(0, DECAY_AT, group * PIX), DECAY_AT, SHARED]
    sends = [
        pltpu.make_async_copy(shared.at[pl.ds(at, to - at)], shared_hbm.at[pl.ds(at, to - at)], out_sem.at[i])
        for i, (at, to) in enumerate(zip(edges[:-1], edges[1:], strict=True))
    ]
    for copy in [small[0], *frames[:2], *copies, small[1], *frames[2:]]:
        copy.start()
    xpad[:, 0] = jnp.zeros((FRAMES, COLS, CIN), BF16)
    xpad[:, ROWS + 1] = jnp.zeros((FRAMES, COLS, CIN), BF16)
    small[0].wait()
    decay = decay_of(codes[...])
    shared[DECAY_AT:WEIGHT_AT] = jnp.broadcast_to(decay, (8, PD))
    for copy in copies:
        copy.wait()
    running = jnp.zeros((PIX, PD), F32)
    for first in range(0, FRAMES, group):
        total = jnp.zeros((group * PIX, 3 * PD), F32)
        for copy in frames[first : first + group]:
            copy.wait()
        for di in range(3):
            rows = xpad[first : first + group, di : di + ROWS].reshape(group * PIX, CIN)
            total = total + jnp.dot(rows, wcat[di], preferred_element_type=F32)
        drive = shifted_sum(total[:, :PD], total[:, PD : 2 * PD], total[:, 2 * PD :])
        for k in range(group):
            running = decay * running + drive[k * PIX : (k + 1) * PIX]
            shared[(first + k) * PIX : (first + k + 1) * PIX] = running
        sends[first // group].start()
        if first == 0:
            small[1].wait()
            for tap in range(9):
                for half in range(2):
                    at = WEIGHT_AT + (2 * tap + half) * PD
                    shared[at : at + PD] = wout[tap // 3, tap % 3, :, half * PD : (half + 1) * PD].astype(F32)
            sends[-1].start()
    end_ref[...] = running.reshape(8, PIX // 8, PD)
    for copy in sends:
        copy.wait()


def total_kernel(ends_ref, codes_ref, out_ref):
    a8 = pow8(decay_of(codes_ref[...]))
    total = ends_ref[0]
    for z in range(1, 8):
        total = a8 * total + ends_ref[z]
    for y in range(8):
        out_ref[y] = total


def mix_kernel(own_ref, first_ref, second_ref, third_ref, out_ref):
    value = own_ref[...] + first_ref[...] + second_ref[...] + third_ref[...]
    half = 0.5 * value
    mixed = half + half * lax.erf(value * (0.5**0.5))
    out_ref[...] = mixed.astype(BF16)


def carry_kernel(ends_ref, totals_ref, codes_ref, wout_ref, other_ref, out_ref, w_ref):
    a8 = pow8(decay_of(codes_ref[...]))
    a64 = pow8(a8)
    own = lax.axis_index("y")
    carry = jnp.zeros((PIX // 8, PD), F32)
    for y in range(8):
        carry = jnp.where(y < own, a64 * carry + totals_ref[y], carry)
    for z in range(8):
        out_ref[z] = carry
        carry = a8 * carry + ends_ref[z]
    w_ref[:, :, :PD] = wout_ref[...]
    for tap in range(9):
        for half in range(2):
            at = WEIGHT_AT + (2 * tap + half) * PD
            w_ref[tap // 3, tap % 3, PD:, half * PD : (half + 1) * PD] = other_ref[at : at + PD].astype(BF16)


def readout(offset, own_ref, other_ref, codes_ref, carry_ref, carry_other_ref, w_ref, spad):
    chip = (lax.axis_index("x") + offset) % 4
    above = 4 * chip + 2 * lax.axis_index("c") - 1
    sides = (
        (own_ref, carry_ref, decay_of(codes_ref[...])),
        (other_ref, carry_other_ref, other_ref[DECAY_AT : DECAY_AT + 1]),
    )
    for row in range(4):
        inside = jnp.logical_and(above + row >= 0, above + row < ROWS)
        at = jnp.clip(above + row, 0, ROWS - 1)
        for side, (ref, carried, decay) in enumerate(sides):
            half = pl.ds(pl.multiple_of(at % 2 * COLS, COLS), COLS)
            carry = jnp.where(inside, carried[at // 2, half], 0.0)
            for j in range(FRAMES):
                carry = decay * carry
                state = ref[pl.ds(pl.multiple_of(at * COLS + j * PIX, COLS), COLS)]
                state = jnp.where(inside, state, 0.0) + carry
                spad[j, row, :, side * PD : (side + 1) * PD] = state.astype(BF16)
    rows = [spad[:, di : di + 2].reshape(FRAMES * 2 * COLS, 2 * PD) for di in range(3)]
    taps = []
    for dj in range(3):
        total = jnp.dot(rows[0], w_ref[0, dj], preferred_element_type=F32)
        for di in range(1, 3):
            total = total + jnp.dot(rows[di], w_ref[di, dj], preferred_element_type=F32)
        taps.append(total)
    return shifted_sum(*taps)


def far_kernel(offset, own_ref, other_ref, codes_ref, carry_ref, carry_other_ref, w_ref, after_ref, out_ref, spad):
    out_ref[...] = readout(offset, own_ref, other_ref, codes_ref, carry_ref, carry_other_ref, w_ref, spad)


def near_kernel(own_ref, other_ref, codes_ref, carry_ref, carry_other_ref, w_ref, after_ref, x_hbm, gain_ref,
                out_ref, spad, frames, sem):
    start = 4 * lax.axis_index("x") + 2 * lax.axis_index("c")
    copy = pltpu.make_async_copy(x_hbm.at[:, pl.ds(start, 2)], frames, sem)
    copy.start()
    value = readout(0, own_ref, other_ref, codes_ref, carry_ref, carry_other_ref, w_ref, spad)
    copy.wait()
    out_ref[...] = value + frames[...].reshape(FRAMES * 2 * COLS, CIN).astype(F32) * gain_ref[...]


def call(kernel, out, args, spaces=None, scratch=(), flops=0, moved=1 << 20, limit=24, outs=None):
    return pl.pallas_call(
        kernel,
        out_shape=out,
        in_specs=[pl.BlockSpec(memory_space=space) for space in spaces or [pltpu.VMEM] * len(args)],
        out_specs=outs or jax.tree.map(lambda _: pl.BlockSpec(memory_space=pltpu.VMEM), out),
        scratch_shapes=list(scratch),
        compiler_params=pltpu.CompilerParams(vmem_limit_bytes=limit << 20),
        cost_estimate=pl.CostEstimate(flops=flops, bytes_accessed=moved, transcendentals=0),
    )(*args)


def shape(*dims, dtype=F32):
    return jax.ShapeDtypeStruct(dims, dtype)


def per_device(frames, in_weight, decay_codes, out_weight, skip_gain):
    codes = decay_codes.reshape(1, PD)
    flops = 2 * FRAMES * PIX * 9 * CIN * PD
    slices = shape(8, PIX // 8, PD)
    owned = FRAMES * 2 * COLS
    shared, end = call(
        drive_kernel,
        (shape(SHARED, PD), slices),
        (frames, in_weight, codes, out_weight),
        spaces=[pltpu.HBM] * 4,
        scratch=(
            pltpu.VMEM((FRAMES, ROWS + 2, COLS, CIN), BF16),
            pltpu.VMEM((3, CIN, 3 * PD), BF16),
            pltpu.VMEM((3, 3, PD, CIN), BF16),
            pltpu.VMEM((1, PD), jnp.int32),
            pltpu.VMEM((SHARED, PD), F32),
            pltpu.SemaphoreType.DMA((FRAMES,)),
            pltpu.SemaphoreType.DMA((9,)),
            pltpu.SemaphoreType.DMA((2,)),
            pltpu.SemaphoreType.DMA((5,)),
        ),
        flops=flops,
        moved=3 << 20,
        limit=59,
        outs=tuple(pl.BlockSpec(memory_space=space) for space in (pltpu.HBM, pltpu.VMEM)),
    )
    swap = [(0, 1), (1, 0)]
    ends = lax.all_to_all(end, "z", 0, 0, tiled=True)
    other = lax.ppermute(shared, "c", swap)
    total = call(total_kernel, slices, (ends, codes))
    totals = lax.all_to_all(total, "y", 0, 0, tiled=True)
    carries, weights = call(
        carry_kernel,
        (slices, shape(3, 3, 2 * PD, CIN, dtype=BF16)),
        (ends, totals, codes, out_weight, other),
    )
    carry = lax.all_to_all(carries, "z", 0, 0, tiled=True)
    carry_other = lax.ppermute(carry, "c", swap)
    inputs = (shared, other, codes, carry, carry_other, weights)
    padded = pltpu.VMEM((FRAMES, 4, COLS, 2 * PD), BF16)
    piece, arrived = carry_other, []
    for offset in (2, 1, 3):
        piece = call(
            functools.partial(far_kernel, offset),
            shape(owned, CIN),
            (*inputs, piece),
            spaces=[pltpu.VMEM] * 6 + [pl.ANY],
            scratch=(padded,),
            flops=flops // 4,
        )
        arrived.append(lax.ppermute(piece, "x", [(i, (i + offset) % 4) for i in range(4)]))
    own = call(
        near_kernel,
        shape(owned, CIN),
        (*inputs, piece, frames, skip_gain.reshape(1, CIN)),
        spaces=[pltpu.VMEM] * 6 + [pl.ANY, pltpu.HBM, pltpu.VMEM],
        scratch=(padded, pltpu.VMEM((FRAMES, 2, COLS, CIN), BF16), pltpu.SemaphoreType.DMA),
        flops=flops // 4,
    )
    mixed = call(mix_kernel, shape(owned, CIN, dtype=BF16), (own, *arrived))
    return mixed.reshape(FRAMES, 2, COLS, CIN)


def solution(mesh):
    finer = Mesh(mesh.devices.reshape(8, 8, 4, 2), ("y", "z", "x", "c"))
    chan = ("x", "c")
    placed = (
        P(("y", "z"), None, None, None),
        P(None, None, None, chan),
        P(chan),
        P(None, None, chan, None),
        P(),
    )
    return jax.shard_map(
        per_device,
        mesh=finer,
        in_specs=placed,
        out_specs=P(("y", "z"), chan, None, None),
        check_vma=False,
    )
```

```python
import functools


import jax
import jax.numpy as jnp
from jax import lax
from jax.experimental import pallas as pl
from jax.experimental.pallas import tpu as pltpu
from jax.sharding import Mesh
from jax.sharding import PartitionSpec as P

FRAMES, ROWS, COLS, CIN, PD = 8, 16, 16, 256, 128
PIX = ROWS * COLS
DECAY_AT = FRAMES * PIX
WEIGHT_AT = DECAY_AT + 8
SHARED = WEIGHT_AT + 18 * PD
ORDER = (1, 3, 2)
F32, BF16 = jnp.float32, jnp.bfloat16


def decay_of(codes):
    return 1.0 - codes.astype(F32) / 4096.0


def pow8(value):
    value = value * value
    value = value * value
    return value * value


def shifted_sum(left, centre, right):
    count = left.shape[0]
    column = lax.broadcasted_iota(jnp.int32, left.shape, 0) % COLS
    from_left = jnp.where(column == 0, 0.0, pltpu.roll(left, 1, 0))
    from_right = jnp.where(column == COLS - 1, 0.0, pltpu.roll(right, count - 1, 0))
    return from_left + centre + from_right


def drive_kernel(x_hbm, w_hbm, codes_hbm, wout_hbm, shared_hbm, end_hbm,
                 xpad, wcat, wout, codes, shared, frame_sem, tap_sem, small_sem, out_sem):
    taps = [(di, dj) for di in range(3) for dj in range(3)]
    copies = [
        pltpu.make_async_copy(w_hbm.at[di, dj], wcat.at[di, :, pl.ds(dj * PD, PD)], tap_sem.at[3 * di + dj])
        for di, dj in taps
    ]
    frames = [
        pltpu.make_async_copy(x_hbm.at[j], xpad.at[j, pl.ds(1, ROWS)], frame_sem.at[j]) for j in range(FRAMES)
    ]
    small = [
        pltpu.make_async_copy(src, dst, small_sem.at[i])
        for i, (src, dst) in enumerate(((codes_hbm, codes), (wout_hbm, wout)))
    ]
    group = 2
    edges = [*range(0, DECAY_AT, group * PIX), DECAY_AT, SHARED]
    sends = [
        pltpu.make_async_copy(shared.at[pl.ds(at, to - at)], shared_hbm.at[pl.ds(at, to - at)], out_sem.at[i])
        for i, (at, to) in enumerate(zip(edges[:-1], edges[1:], strict=True))
    ]
    last, part = DECAY_AT - PIX, PIX // 8
    ends = [
        pltpu.make_async_copy(shared.at[pl.ds(last + i * part, part)], end_hbm.at[i], out_sem.at[len(sends) + i])
        for i in range(8)
    ]
    for copy in [small[0], *frames[:group], *copies, *frames[group:], small[1]]:
        copy.start()
    xpad[:, 0] = jnp.zeros((FRAMES, COLS, CIN), BF16)
    xpad[:, ROWS + 1] = jnp.zeros((FRAMES, COLS, CIN), BF16)
    small[0].wait()
    decay = decay_of(codes[...])
    shared[DECAY_AT:WEIGHT_AT] = jnp.broadcast_to(decay, (8, PD))
    running = jnp.zeros((PIX, PD), F32)
    for first in range(0, FRAMES, group):
        total = jnp.zeros((group * PIX, 3 * PD), F32)
        for copy in frames[first : first + group]:
            copy.wait()
        for di in range(3):
            if first == 0:
                for copy in copies[3 * di : 3 * di + 3]:
                    copy.wait()
            rows = xpad[first : first + group, di : di + ROWS].reshape(group * PIX, CIN)
            total = total + jnp.dot(rows, wcat[di], preferred_element_type=F32)
        drive = shifted_sum(total[:, :PD], total[:, PD : 2 * PD], total[:, 2 * PD :])
        for k in range(group):
            running = decay * running + drive[k * PIX : (k + 1) * PIX]
            shared[(first + k) * PIX : (first + k + 1) * PIX] = running
        if first + group == FRAMES:
            for copy in ends:
                copy.start()
        sends[first // group].start()
        if first == FRAMES // 2:
            small[1].wait()
            for tap in range(9):
                for half in range(2):
                    at = WEIGHT_AT + (2 * tap + half) * PD
                    shared[at : at + PD] = wout[tap // 3, tap % 3, :, half * PD : (half + 1) * PD].astype(F32)
            sends[-1].start()
    for copy in ends + sends:
        copy.wait()


def total_kernel(ends_ref, codes_ref, out_ref):
    a8 = pow8(decay_of(codes_ref[...]))
    total = ends_ref[0]
    for z in range(1, 8):
        total = a8 * total + ends_ref[z]
    for y in range(8):
        out_ref[y] = total


def mix_kernel(own_ref, first_ref, second_ref, third_ref, out_ref):
    value = own_ref[...] + first_ref[...] + second_ref[...] + third_ref[...]
    half = 0.5 * value
    mixed = half + half * lax.erf(value * (0.5**0.5))
    out_ref[...] = mixed.astype(BF16)


def carry_kernel(ends_ref, totals_ref, codes_ref, wout_ref, other_ref, out_ref, w_ref):
    a8 = pow8(decay_of(codes_ref[...]))
    a64 = pow8(a8)
    own = lax.axis_index("y")
    carry = jnp.zeros((PIX // 8, PD), F32)
    for y in range(8):
        carry = jnp.where(y < own, a64 * carry + totals_ref[y], carry)
    for z in range(8):
        out_ref[z] = carry
        carry = a8 * carry + ends_ref[z]
    w_ref[:, :, :PD] = wout_ref[...]
    for tap in range(9):
        for half in range(2):
            at = WEIGHT_AT + (2 * tap + half) * PD
            w_ref[tap // 3, tap % 3, PD:, half * PD : (half + 1) * PD] = other_ref[at : at + PD].astype(BF16)


def readout(offset, own_ref, other_ref, codes_ref, carry_ref, carry_other_ref, w_ref, spad):
    chip = lax.axis_index("x") ^ offset
    above = 4 * chip + 2 * lax.axis_index("c") - 1
    sides = (
        (own_ref, carry_ref, decay_of(codes_ref[...])),
        (other_ref, carry_other_ref, other_ref[DECAY_AT : DECAY_AT + 1]),
    )
    for row in range(4):
        inside = jnp.logical_and(above + row >= 0, above + row < ROWS)
        at = jnp.clip(above + row, 0, ROWS - 1)
        for side, (ref, carried, decay) in enumerate(sides):
            half = pl.ds(pl.multiple_of(at % 2 * COLS, COLS), COLS)
            carry = jnp.where(inside, carried[at // 2, half], 0.0)
            for j in range(FRAMES):
                carry = decay * carry
                state = ref[pl.ds(pl.multiple_of(at * COLS + j * PIX, COLS), COLS)]
                state = jnp.where(inside, state, 0.0) + carry
                spad[j, row, :, side * PD : (side + 1) * PD] = state.astype(BF16)
    rows = [spad[:, di : di + 2].reshape(FRAMES * 2 * COLS, 2 * PD) for di in range(3)]
    taps = []
    for dj in range(3):
        total = jnp.dot(rows[0], w_ref[0, dj], preferred_element_type=F32)
        for di in range(1, 3):
            total = total + jnp.dot(rows[di], w_ref[di, dj], preferred_element_type=F32)
        taps.append(total)
    return shifted_sum(*taps)


def far_kernel(offset, own_ref, other_ref, codes_ref, carry_ref, carry_other_ref, w_ref, after_ref, out_ref, spad):
    out_ref[...] = readout(offset, own_ref, other_ref, codes_ref, carry_ref, carry_other_ref, w_ref, spad)


def near_kernel(own_ref, other_ref, codes_ref, carry_ref, carry_other_ref, w_ref, after_ref, x_hbm, gain_ref,
                out_ref, spad, frames, sem):
    start = 4 * lax.axis_index("x") + 2 * lax.axis_index("c")
    copy = pltpu.make_async_copy(x_hbm.at[:, pl.ds(start, 2)], frames, sem)
    copy.start()
    value = readout(0, own_ref, other_ref, codes_ref, carry_ref, carry_other_ref, w_ref, spad)
    copy.wait()
    out_ref[...] = value + frames[...].reshape(FRAMES * 2 * COLS, CIN).astype(F32) * gain_ref[...]


def call(kernel, out, args, spaces=None, scratch=(), flops=0, moved=1 << 20, limit=24, outs=None):
    return pl.pallas_call(
        kernel,
        out_shape=out,
        in_specs=[pl.BlockSpec(memory_space=space) for space in spaces or [pltpu.VMEM] * len(args)],
        out_specs=outs or jax.tree.map(lambda _: pl.BlockSpec(memory_space=pltpu.VMEM), out),
        scratch_shapes=list(scratch),
        compiler_params=pltpu.CompilerParams(vmem_limit_bytes=limit << 20),
        cost_estimate=pl.CostEstimate(flops=flops, bytes_accessed=moved, transcendentals=0),
    )(*args)


def shape(*dims, dtype=F32):
    return jax.ShapeDtypeStruct(dims, dtype)


def per_device(frames, in_weight, decay_codes, out_weight, skip_gain):
    codes = decay_codes.reshape(1, PD)
    flops = 2 * FRAMES * PIX * 9 * CIN * PD
    slices = shape(8, PIX // 8, PD)
    owned = FRAMES * 2 * COLS
    shared, end = call(
        drive_kernel,
        (shape(SHARED, PD), slices),
        (frames, in_weight, codes, out_weight),
        spaces=[pltpu.HBM] * 4,
        scratch=(
            pltpu.VMEM((FRAMES, ROWS + 2, COLS, CIN), BF16),
            pltpu.VMEM((3, CIN, 3 * PD), BF16),
            pltpu.VMEM((3, 3, PD, CIN), BF16),
            pltpu.VMEM((1, PD), jnp.int32),
            pltpu.VMEM((SHARED, PD), F32),
            pltpu.SemaphoreType.DMA((FRAMES,)),
            pltpu.SemaphoreType.DMA((9,)),
            pltpu.SemaphoreType.DMA((2,)),
            pltpu.SemaphoreType.DMA((13,)),
        ),
        flops=flops,
        moved=3 << 20,
        limit=59,
        outs=tuple(pl.BlockSpec(memory_space=space) for space in (pltpu.HBM, pltpu.HBM)),
    )
    swap = [(0, 1), (1, 0)]
    ends = lax.all_to_all(end, "z", 0, 0, tiled=True)
    other = lax.ppermute(shared, "c", swap)
    total = call(total_kernel, slices, (ends, codes))
    totals = lax.all_to_all(total, "y", 0, 0, tiled=True)
    carries, weights = call(
        carry_kernel,
        (slices, shape(3, 3, 2 * PD, CIN, dtype=BF16)),
        (ends, totals, codes, out_weight, other),
    )
    carry = lax.all_to_all(carries, "z", 0, 0, tiled=True)
    carry_other = lax.ppermute(carry, "c", swap)
    inputs = (shared, other, codes, carry, carry_other, weights)
    padded = pltpu.VMEM((FRAMES, 4, COLS, 2 * PD), BF16)
    piece, arrived = carry_other, []
    for offset in ORDER:
        piece = call(
            functools.partial(far_kernel, offset),
            shape(owned, CIN),
            (*inputs, piece),
            spaces=[pltpu.VMEM] * 6 + [pl.ANY],
            scratch=(padded,),
            flops=flops // 4,
        )
        arrived.append(lax.ppermute(piece, "x", [(i, i ^ offset) for i in range(4)]))
    own = call(
        near_kernel,
        shape(owned, CIN),
        (*inputs, piece, frames, skip_gain.reshape(1, CIN)),
        spaces=[pltpu.VMEM] * 6 + [pl.ANY, pltpu.HBM, pltpu.VMEM],
        scratch=(padded, pltpu.VMEM((FRAMES, 2, COLS, CIN), BF16), pltpu.SemaphoreType.DMA),
        flops=flops // 4,
    )
    mixed = call(mix_kernel, shape(owned, CIN, dtype=BF16), (own, *arrived))
    return mixed.reshape(FRAMES, 2, COLS, CIN)


def solution(mesh):
    finer = Mesh(mesh.devices.reshape(8, 8, 4, 2), ("y", "z", "x", "c"))
    chan = ("x", "c")
    placed = (
        P(("y", "z"), None, None, None),
        P(None, None, None, chan),
        P(chan),
        P(None, None, chan, None),
        P(),
    )
    return jax.shard_map(
        per_device,
        mesh=finer,
        in_specs=placed,
        out_specs=P(("y", "z"), chan, None, None),
        check_vma=False,
    )
```

```python
import functools


import jax
import jax.numpy as jnp
from jax import lax
from jax.experimental import pallas as pl
from jax.experimental.pallas import tpu as pltpu
from jax.sharding import Mesh
from jax.sharding import PartitionSpec as P

FRAMES, ROWS, COLS, CIN, PD = 8, 16, 16, 256, 128
PIX = ROWS * COLS
DECAY_AT = FRAMES * PIX
WEIGHT_AT = DECAY_AT + 8
SHARED = WEIGHT_AT + 18 * PD
ORDER = (2, 1, 3)
F32, BF16 = jnp.float32, jnp.bfloat16


def decay_of(codes):
    return 1.0 - codes.astype(F32) / 4096.0


def pow8(value):
    value = value * value
    value = value * value
    return value * value


def shifted_sum(left, centre, right):
    count = left.shape[0]
    column = lax.broadcasted_iota(jnp.int32, left.shape, 0) % COLS
    from_left = jnp.where(column == 0, 0.0, pltpu.roll(left, 1, 0))
    from_right = jnp.where(column == COLS - 1, 0.0, pltpu.roll(right, count - 1, 0))
    return from_left + centre + from_right


def drive_kernel(x_hbm, w_hbm, codes_hbm, wout_hbm, shared_hbm, end_hbm,
                 xpad, wcat, wout, codes, shared, frame_sem, tap_sem, small_sem, out_sem):
    taps = [(di, dj) for di in range(3) for dj in range(3)]
    copies = [
        pltpu.make_async_copy(w_hbm.at[di, dj], wcat.at[di, :, pl.ds(dj * PD, PD)], tap_sem.at[3 * di + dj])
        for di, dj in taps
    ]
    frames = [
        pltpu.make_async_copy(x_hbm.at[j], xpad.at[j, pl.ds(1, ROWS)], frame_sem.at[j]) for j in range(FRAMES)
    ]
    small = [
        pltpu.make_async_copy(src, dst, small_sem.at[i])
        for i, (src, dst) in enumerate(((codes_hbm, codes), (wout_hbm, wout)))
    ]
    group = FRAMES // 2
    edges = [*range(0, DECAY_AT, PIX), DECAY_AT, SHARED]
    sends = [
        pltpu.make_async_copy(shared.at[pl.ds(at, to - at)], shared_hbm.at[pl.ds(at, to - at)], out_sem.at[i])
        for i, (at, to) in enumerate(zip(edges[:-1], edges[1:], strict=True))
    ]
    last, part = DECAY_AT - PIX, PIX // 8
    ends = [
        pltpu.make_async_copy(shared.at[pl.ds(last + i * part, part)], end_hbm.at[i], out_sem.at[len(sends) + i])
        for i in range(8)
    ]
    for copy in [small[0], *copies[:3], *frames[:group], *copies[3:], *frames[group:], small[1]]:
        copy.start()
    xpad[:, 0] = jnp.zeros((FRAMES, COLS, CIN), BF16)
    xpad[:, ROWS + 1] = jnp.zeros((FRAMES, COLS, CIN), BF16)
    small[0].wait()
    decay = decay_of(codes[...])
    shared[DECAY_AT:WEIGHT_AT] = jnp.broadcast_to(decay, (8, PD))
    running = jnp.zeros((PIX, PD), F32)
    for first in range(0, FRAMES, group):
        for copy in frames[first : first + group]:
            copy.wait()
        total = jnp.zeros((group * PIX, 3 * PD), F32)
        for di in range(3):
            if first == 0:
                for copy in copies[3 * di : 3 * di + 3]:
                    copy.wait()
            rows = xpad[first : first + group, di : di + ROWS].reshape(group * PIX, CIN)
            total = total + jnp.dot(rows, wcat[di], preferred_element_type=F32)
        drive = shifted_sum(total[:, :PD], total[:, PD : 2 * PD], total[:, 2 * PD :])
        for k in range(group):
            frame = first + k
            running = decay * running + drive[k * PIX : (k + 1) * PIX]
            shared[frame * PIX : (frame + 1) * PIX] = running
            if frame < FRAMES - 1:
                sends[frame].start()
        if first == 0:
            small[1].wait()
            for tap in range(9):
                for half in range(2):
                    at = WEIGHT_AT + (2 * tap + half) * PD
                    shared[at : at + PD] = wout[tap // 3, tap % 3, :, half * PD : (half + 1) * PD].astype(F32)
            sends[-1].start()
    for copy in ends:
        copy.start()
    sends[FRAMES - 1].start()
    for copy in ends + sends:
        copy.wait()


def total_kernel(ends_ref, codes_ref, out_ref):
    a8 = pow8(decay_of(codes_ref[...]))
    total = ends_ref[0]
    for z in range(1, 8):
        total = a8 * total + ends_ref[z]
    for y in range(8):
        out_ref[y] = total


def mix_kernel(own_ref, first_ref, second_ref, third_ref, out_ref):
    value = own_ref[...] + first_ref[...] + second_ref[...] + third_ref[...]
    half = 0.5 * value
    mixed = half + half * lax.erf(value * (0.5**0.5))
    out_ref[...] = mixed.astype(BF16)


def carry_kernel(ends_ref, totals_ref, codes_ref, wout_ref, other_ref, out_ref, w_ref):
    a8 = pow8(decay_of(codes_ref[...]))
    a64 = pow8(a8)
    own = lax.axis_index("y")
    carry = jnp.zeros((PIX // 8, PD), F32)
    for y in range(8):
        carry = jnp.where(y < own, a64 * carry + totals_ref[y], carry)
    for z in range(8):
        out_ref[z] = carry
        carry = a8 * carry + ends_ref[z]
    w_ref[:, :, :PD] = wout_ref[...]
    for tap in range(9):
        for half in range(2):
            at = WEIGHT_AT + (2 * tap + half) * PD
            w_ref[tap // 3, tap % 3, PD:, half * PD : (half + 1) * PD] = other_ref[at : at + PD].astype(BF16)


def readout(offset, own_ref, other_ref, codes_ref, carry_ref, carry_other_ref, w_ref, spad):
    chip = (lax.axis_index("x") + offset) % 4
    above = 4 * chip + 2 * lax.axis_index("c") - 1
    sides = (
        (own_ref, carry_ref, decay_of(codes_ref[...])),
        (other_ref, carry_other_ref, other_ref[DECAY_AT : DECAY_AT + 1]),
    )
    for row in range(4):
        inside = jnp.logical_and(above + row >= 0, above + row < ROWS)
        at = jnp.clip(above + row, 0, ROWS - 1)
        for side, (ref, carried, decay) in enumerate(sides):
            half = pl.ds(pl.multiple_of(at % 2 * COLS, COLS), COLS)
            carry = jnp.where(inside, carried[at // 2, half], 0.0)
            for j in range(FRAMES):
                carry = decay * carry
                state = ref[pl.ds(pl.multiple_of(at * COLS + j * PIX, COLS), COLS)]
                state = jnp.where(inside, state, 0.0) + carry
                spad[j, row, :, side * PD : (side + 1) * PD] = state.astype(BF16)
    rows = [spad[:, di : di + 2].reshape(FRAMES * 2 * COLS, 2 * PD) for di in range(3)]
    taps = []
    for dj in range(3):
        total = jnp.dot(rows[0], w_ref[0, dj], preferred_element_type=F32)
        for di in range(1, 3):
            total = total + jnp.dot(rows[di], w_ref[di, dj], preferred_element_type=F32)
        taps.append(total)
    return shifted_sum(*taps)


def far_kernel(offset, own_ref, other_ref, codes_ref, carry_ref, carry_other_ref, w_ref, after_ref, out_ref, spad):
    out_ref[...] = readout(offset, own_ref, other_ref, codes_ref, carry_ref, carry_other_ref, w_ref, spad)


def near_kernel(own_ref, other_ref, codes_ref, carry_ref, carry_other_ref, w_ref, after_ref, x_hbm, gain_ref,
                out_ref, spad, frames, sem):
    start = 4 * lax.axis_index("x") + 2 * lax.axis_index("c")
    copy = pltpu.make_async_copy(x_hbm.at[:, pl.ds(start, 2)], frames, sem)
    copy.start()
    value = readout(0, own_ref, other_ref, codes_ref, carry_ref, carry_other_ref, w_ref, spad)
    copy.wait()
    out_ref[...] = value + frames[...].reshape(FRAMES * 2 * COLS, CIN).astype(F32) * gain_ref[...]


def call(kernel, out, args, spaces=None, scratch=(), flops=0, moved=1 << 20, limit=24, outs=None):
    return pl.pallas_call(
        kernel,
        out_shape=out,
        in_specs=[pl.BlockSpec(memory_space=space) for space in spaces or [pltpu.VMEM] * len(args)],
        out_specs=outs or jax.tree.map(lambda _: pl.BlockSpec(memory_space=pltpu.VMEM), out),
        scratch_shapes=list(scratch),
        compiler_params=pltpu.CompilerParams(vmem_limit_bytes=limit << 20),
        cost_estimate=pl.CostEstimate(flops=flops, bytes_accessed=moved, transcendentals=0),
    )(*args)


def shape(*dims, dtype=F32):
    return jax.ShapeDtypeStruct(dims, dtype)


def per_device(frames, in_weight, decay_codes, out_weight, skip_gain):
    codes = decay_codes.reshape(1, PD)
    flops = 2 * FRAMES * PIX * 9 * CIN * PD
    slices = shape(8, PIX // 8, PD)
    owned = FRAMES * 2 * COLS
    shared, end = call(
        drive_kernel,
        (shape(SHARED, PD), slices),
        (frames, in_weight, codes, out_weight),
        spaces=[pltpu.HBM] * 4,
        scratch=(
            pltpu.VMEM((FRAMES, ROWS + 2, COLS, CIN), BF16),
            pltpu.VMEM((3, CIN, 3 * PD), BF16),
            pltpu.VMEM((3, 3, PD, CIN), BF16),
            pltpu.VMEM((1, PD), jnp.int32),
            pltpu.VMEM((SHARED, PD), F32),
            pltpu.SemaphoreType.DMA((FRAMES,)),
            pltpu.SemaphoreType.DMA((9,)),
            pltpu.SemaphoreType.DMA((2,)),
            pltpu.SemaphoreType.DMA((17,)),
        ),
        flops=flops,
        moved=3 << 20,
        limit=59,
        outs=tuple(pl.BlockSpec(memory_space=space) for space in (pltpu.HBM, pltpu.HBM)),
    )
    swap = [(0, 1), (1, 0)]
    ends = lax.all_to_all(end, "z", 0, 0, tiled=True)
    other = lax.ppermute(shared, "c", swap)
    total = call(total_kernel, slices, (ends, codes))
    totals = lax.all_to_all(total, "y", 0, 0, tiled=True)
    carries, weights = call(
        carry_kernel,
        (slices, shape(3, 3, 2 * PD, CIN, dtype=BF16)),
        (ends, totals, codes, out_weight, other),
    )
    carry = lax.all_to_all(carries, "z", 0, 0, tiled=True)
    carry_other = lax.ppermute(carry, "c", swap)
    inputs = (shared, other, codes, carry, carry_other, weights)
    padded = pltpu.VMEM((FRAMES, 4, COLS, 2 * PD), BF16)
    piece, arrived = carry_other, []
    for offset in ORDER:
        piece = call(
            functools.partial(far_kernel, offset),
            shape(owned, CIN),
            (*inputs, piece),
            spaces=[pltpu.VMEM] * 6 + [pl.ANY],
            scratch=(padded,),
            flops=flops // 4,
        )
        arrived.append(lax.ppermute(piece, "x", [(i, (i + offset) % 4) for i in range(4)]))
    own = call(
        near_kernel,
        shape(owned, CIN),
        (*inputs, piece, frames, skip_gain.reshape(1, CIN)),
        spaces=[pltpu.VMEM] * 6 + [pl.ANY, pltpu.HBM, pltpu.VMEM],
        scratch=(padded, pltpu.VMEM((FRAMES, 2, COLS, CIN), BF16), pltpu.SemaphoreType.DMA),
        flops=flops // 4,
    )
    mixed = call(mix_kernel, shape(owned, CIN, dtype=BF16), (own, *arrived))
    return mixed.reshape(FRAMES, 2, COLS, CIN)


def solution(mesh):
    finer = Mesh(mesh.devices.reshape(8, 8, 4, 2), ("y", "z", "x", "c"))
    chan = ("x", "c")
    placed = (
        P(("y", "z"), None, None, None),
        P(None, None, None, chan),
        P(chan),
        P(None, None, chan, None),
        P(),
    )
    return jax.shard_map(
        per_device,
        mesh=finer,
        in_specs=placed,
        out_specs=P(("y", "z"), chan, None, None),
        check_vma=False,
    )
```

```python
import functools


import jax
import jax.numpy as jnp
from jax import lax
from jax.experimental import pallas as pl
from jax.experimental.pallas import tpu as pltpu
from jax.sharding import Mesh
from jax.sharding import PartitionSpec as P

FRAMES, ROWS, COLS, CIN, PD = 8, 16, 16, 256, 128
PIX = ROWS * COLS
DECAY_AT = FRAMES * PIX
WEIGHT_AT = DECAY_AT + 8
SHARED = WEIGHT_AT + 18 * PD
ORDER = (2, 1, 3)
F32, BF16 = jnp.float32, jnp.bfloat16


def decay_of(codes):
    return 1.0 - codes.astype(F32) / 4096.0


def pow8(value):
    value = value * value
    value = value * value
    return value * value


def shifted_sum(left, centre, right):
    count = left.shape[0]
    column = lax.broadcasted_iota(jnp.int32, left.shape, 0) % COLS
    from_left = jnp.where(column == 0, 0.0, pltpu.roll(left, 1, 0))
    from_right = jnp.where(column == COLS - 1, 0.0, pltpu.roll(right, count - 1, 0))
    return from_left + centre + from_right


def drive_kernel(x_hbm, w_hbm, codes_hbm, wout_hbm, shared_hbm, end_hbm,
                 xpad, wcat, wout, codes, shared, frame_sem, tap_sem, small_sem, out_sem):
    taps = [(di, dj) for di in range(3) for dj in range(3)]
    copies = [
        pltpu.make_async_copy(w_hbm.at[di, dj], wcat.at[di, :, pl.ds(dj * PD, PD)], tap_sem.at[3 * di + dj])
        for di, dj in taps
    ]
    frames = [
        pltpu.make_async_copy(x_hbm.at[j], xpad.at[j, pl.ds(1, ROWS)], frame_sem.at[j]) for j in range(FRAMES)
    ]
    small = [
        pltpu.make_async_copy(src, dst, small_sem.at[i])
        for i, (src, dst) in enumerate(((codes_hbm, codes), (wout_hbm, wout)))
    ]
    group = FRAMES // 2
    edges = [*range(0, DECAY_AT, PIX), DECAY_AT, SHARED]
    sends = [
        pltpu.make_async_copy(shared.at[pl.ds(at, to - at)], shared_hbm.at[pl.ds(at, to - at)], out_sem.at[i])
        for i, (at, to) in enumerate(zip(edges[:-1], edges[1:], strict=True))
    ]
    last, part = DECAY_AT - PIX, PIX // 8
    ends = [
        pltpu.make_async_copy(shared.at[pl.ds(last + i * part, part)], end_hbm.at[i], out_sem.at[len(sends) + i])
        for i in range(8)
    ]
    for copy in [small[0], *copies[:3], *frames[:group], *copies[3:], *frames[group:], small[1]]:
        copy.start()
    xpad[:, 0] = jnp.zeros((FRAMES, COLS, CIN), BF16)
    xpad[:, ROWS + 1] = jnp.zeros((FRAMES, COLS, CIN), BF16)
    small[0].wait()
    decay = decay_of(codes[...])
    shared[DECAY_AT:WEIGHT_AT] = jnp.broadcast_to(decay, (8, PD))
    running = jnp.zeros((PIX, PD), F32)
    for first in range(0, FRAMES, group):
        for copy in frames[first : first + group]:
            copy.wait()
        total = jnp.zeros((group * PIX, 3 * PD), F32)
        for di in range(3):
            if first == 0:
                for copy in copies[3 * di : 3 * di + 3]:
                    copy.wait()
            rows = xpad[first : first + group, di : di + ROWS].reshape(group * PIX, CIN)
            total = total + jnp.dot(rows, wcat[di], preferred_element_type=F32)
        drive = shifted_sum(total[:, :PD], total[:, PD : 2 * PD], total[:, 2 * PD :])
        for k in range(group):
            frame = first + k
            running = decay * running + drive[k * PIX : (k + 1) * PIX]
            shared[frame * PIX : (frame + 1) * PIX] = running
            if frame < FRAMES - 1:
                sends[frame].start()
        if first == 0:
            small[1].wait()
            for tap in range(9):
                for half in range(2):
                    at = WEIGHT_AT + (2 * tap + half) * PD
                    shared[at : at + PD] = wout[tap // 3, tap % 3, :, half * PD : (half + 1) * PD].astype(F32)
            sends[-1].start()
    for copy in ends:
        copy.start()
    sends[FRAMES - 1].start()
    for copy in ends + sends:
        copy.wait()


def total_kernel(ends_ref, codes_ref, out_ref):
    a8 = pow8(decay_of(codes_ref[...]))
    total = ends_ref[0]
    for z in range(1, 8):
        total = a8 * total + ends_ref[z]
    for y in range(8):
        out_ref[y] = total


def mix_kernel(own_ref, first_ref, second_ref, third_ref, out_ref):
    value = own_ref[...] + first_ref[...] + second_ref[...] + third_ref[...]
    half = 0.5 * value
    mixed = half + half * lax.erf(value * (0.5**0.5))
    out_ref[...] = mixed.astype(BF16)


def carry_kernel(ends_ref, totals_ref, codes_ref, wout_ref, other_ref, out_ref, w_ref):
    a8 = pow8(decay_of(codes_ref[...]))
    a64 = pow8(a8)
    own = lax.axis_index("y")
    carry = jnp.zeros((PIX // 8, PD), F32)
    for y in range(8):
        carry = jnp.where(y < own, a64 * carry + totals_ref[y], carry)
    for z in range(8):
        out_ref[z] = carry
        carry = a8 * carry + ends_ref[z]
    w_ref[:, :, :PD] = wout_ref[...]
    for tap in range(9):
        for half in range(2):
            at = WEIGHT_AT + (2 * tap + half) * PD
            w_ref[tap // 3, tap % 3, PD:, half * PD : (half + 1) * PD] = other_ref[at : at + PD].astype(BF16)


def readout(offset, own_ref, other_ref, codes_ref, carry_ref, carry_other_ref, w_ref, spad):
    chip = (lax.axis_index("x") + offset + 2 * offset * lax.axis_index("c")) % 4
    above = 4 * chip + 2 * lax.axis_index("c") - 1
    sides = (
        (own_ref, carry_ref, decay_of(codes_ref[...])),
        (other_ref, carry_other_ref, other_ref[DECAY_AT : DECAY_AT + 1]),
    )
    for row in range(4):
        inside = jnp.logical_and(above + row >= 0, above + row < ROWS)
        at = jnp.clip(above + row, 0, ROWS - 1)
        for side, (ref, carried, decay) in enumerate(sides):
            half = pl.ds(pl.multiple_of(at % 2 * COLS, COLS), COLS)
            carry = jnp.where(inside, carried[at // 2, half], 0.0)
            for j in range(FRAMES):
                carry = decay * carry
                state = ref[pl.ds(pl.multiple_of(at * COLS + j * PIX, COLS), COLS)]
                state = jnp.where(inside, state, 0.0) + carry
                spad[j, row, :, side * PD : (side + 1) * PD] = state.astype(BF16)
    rows = [spad[:, di : di + 2].reshape(FRAMES * 2 * COLS, 2 * PD) for di in range(3)]
    taps = []
    for dj in range(3):
        total = jnp.dot(rows[0], w_ref[0, dj], preferred_element_type=F32)
        for di in range(1, 3):
            total = total + jnp.dot(rows[di], w_ref[di, dj], preferred_element_type=F32)
        taps.append(total)
    return shifted_sum(*taps)


def far_kernel(offset, own_ref, other_ref, codes_ref, carry_ref, carry_other_ref, w_ref, after_ref, out_ref, spad):
    out_ref[...] = readout(offset, own_ref, other_ref, codes_ref, carry_ref, carry_other_ref, w_ref, spad)


def near_kernel(own_ref, other_ref, codes_ref, carry_ref, carry_other_ref, w_ref, after_ref, x_hbm, gain_ref,
                out_ref, spad, frames, sem):
    start = 4 * lax.axis_index("x") + 2 * lax.axis_index("c")
    copy = pltpu.make_async_copy(x_hbm.at[:, pl.ds(start, 2)], frames, sem)
    copy.start()
    value = readout(0, own_ref, other_ref, codes_ref, carry_ref, carry_other_ref, w_ref, spad)
    copy.wait()
    out_ref[...] = value + frames[...].reshape(FRAMES * 2 * COLS, CIN).astype(F32) * gain_ref[...]


def call(kernel, out, args, spaces=None, scratch=(), flops=0, moved=1 << 20, limit=24, outs=None):
    return pl.pallas_call(
        kernel,
        out_shape=out,
        in_specs=[pl.BlockSpec(memory_space=space) for space in spaces or [pltpu.VMEM] * len(args)],
        out_specs=outs or jax.tree.map(lambda _: pl.BlockSpec(memory_space=pltpu.VMEM), out),
        scratch_shapes=list(scratch),
        compiler_params=pltpu.CompilerParams(vmem_limit_bytes=limit << 20),
        cost_estimate=pl.CostEstimate(flops=flops, bytes_accessed=moved, transcendentals=0),
    )(*args)


def ahead(offset):
    return [(2 * x + c, 2 * ((x + (1 - 2 * c) * offset) % 4) + c) for x in range(4) for c in range(2)]


def shape(*dims, dtype=F32):
    return jax.ShapeDtypeStruct(dims, dtype)


def per_device(frames, in_weight, decay_codes, out_weight, skip_gain):
    codes = decay_codes.reshape(1, PD)
    flops = 2 * FRAMES * PIX * 9 * CIN * PD
    slices = shape(8, PIX // 8, PD)
    owned = FRAMES * 2 * COLS
    shared, end = call(
        drive_kernel,
        (shape(SHARED, PD), slices),
        (frames, in_weight, codes, out_weight),
        spaces=[pltpu.HBM] * 4,
        scratch=(
            pltpu.VMEM((FRAMES, ROWS + 2, COLS, CIN), BF16),
            pltpu.VMEM((3, CIN, 3 * PD), BF16),
            pltpu.VMEM((3, 3, PD, CIN), BF16),
            pltpu.VMEM((1, PD), jnp.int32),
            pltpu.VMEM((SHARED, PD), F32),
            pltpu.SemaphoreType.DMA((FRAMES,)),
            pltpu.SemaphoreType.DMA((9,)),
            pltpu.SemaphoreType.DMA((2,)),
            pltpu.SemaphoreType.DMA((17,)),
        ),
        flops=flops,
        moved=3 << 20,
        limit=59,
        outs=tuple(pl.BlockSpec(memory_space=space) for space in (pltpu.HBM, pltpu.HBM)),
    )
    swap = [(0, 1), (1, 0)]
    ends = lax.all_to_all(end, "z", 0, 0, tiled=True)
    other = lax.ppermute(shared, "c", swap)
    total = call(total_kernel, slices, (ends, codes))
    totals = lax.all_to_all(total, "y", 0, 0, tiled=True)
    carries, weights = call(
        carry_kernel,
        (slices, shape(3, 3, 2 * PD, CIN, dtype=BF16)),
        (ends, totals, codes, out_weight, other),
    )
    carry = lax.all_to_all(carries, "z", 0, 0, tiled=True)
    carry_other = lax.ppermute(carry, "c", swap)
    inputs = (shared, other, codes, carry, carry_other, weights)
    padded = pltpu.VMEM((FRAMES, 4, COLS, 2 * PD), BF16)
    piece, arrived = carry_other, []
    for offset in ORDER:
        piece = call(
            functools.partial(far_kernel, offset),
            shape(owned, CIN),
            (*inputs, piece),
            spaces=[pltpu.VMEM] * 6 + [pl.ANY],
            scratch=(padded,),
            flops=flops // 4,
        )
        arrived.append(lax.ppermute(piece, ("x", "c"), ahead(offset)))
    own = call(
        near_kernel,
        shape(owned, CIN),
        (*inputs, piece, frames, skip_gain.reshape(1, CIN)),
        spaces=[pltpu.VMEM] * 6 + [pl.ANY, pltpu.HBM, pltpu.VMEM],
        scratch=(padded, pltpu.VMEM((FRAMES, 2, COLS, CIN), BF16), pltpu.SemaphoreType.DMA),
        flops=flops // 4,
    )
    mixed = call(mix_kernel, shape(owned, CIN, dtype=BF16), (own, *arrived))
    return mixed.reshape(FRAMES, 2, COLS, CIN)


def solution(mesh):
    finer = Mesh(mesh.devices.reshape(8, 8, 4, 2), ("y", "z", "x", "c"))
    chan = ("x", "c")
    placed = (
        P(("y", "z"), None, None, None),
        P(None, None, None, chan),
        P(chan),
        P(None, None, chan, None),
        P(),
    )
    return jax.shard_map(
        per_device,
        mesh=finer,
        in_specs=placed,
        out_specs=P(("y", "z"), chan, None, None),
        check_vma=False,
    )
```

```python
import functools


import jax
import jax.numpy as jnp
from jax import lax
from jax.experimental import pallas as pl
from jax.experimental.pallas import tpu as pltpu
from jax.sharding import Mesh
from jax.sharding import PartitionSpec as P

FRAMES, ROWS, COLS, CIN, PD = 8, 16, 16, 256, 128
PIX = ROWS * COLS
DECAY_AT = FRAMES * PIX
WEIGHT_AT = DECAY_AT + 8
SHARED = WEIGHT_AT + 18 * PD
ORDER = (2, 1, 3)
F32, BF16 = jnp.float32, jnp.bfloat16


def decay_of(codes):
    return 1.0 - codes.astype(F32) / 4096.0


def pow8(value):
    value = value * value
    value = value * value
    return value * value


def shifted_sum(left, centre, right):
    count = left.shape[0]
    column = lax.broadcasted_iota(jnp.int32, left.shape, 0) % COLS
    from_left = jnp.where(column == 0, 0.0, pltpu.roll(left, 1, 0))
    from_right = jnp.where(column == COLS - 1, 0.0, pltpu.roll(right, count - 1, 0))
    return from_left + centre + from_right


def drive_kernel(x_hbm, w_hbm, codes_hbm, wout_hbm, shared_hbm, end_hbm,
                 xpad, wcat, wout, codes, shared, frame_sem, tap_sem, small_sem, out_sem):
    taps = [(di, dj) for di in range(3) for dj in range(3)]
    copies = [
        pltpu.make_async_copy(w_hbm.at[di, dj], wcat.at[di, :, pl.ds(dj * PD, PD)], tap_sem.at[3 * di + dj])
        for di, dj in taps
    ]
    frames = [
        pltpu.make_async_copy(x_hbm.at[j], xpad.at[j, pl.ds(1, ROWS)], frame_sem.at[j]) for j in range(FRAMES)
    ]
    small = [
        pltpu.make_async_copy(src, dst, small_sem.at[i])
        for i, (src, dst) in enumerate(((codes_hbm, codes), (wout_hbm, wout)))
    ]
    group = FRAMES // 2
    edges = [*range(0, DECAY_AT, PIX), DECAY_AT, SHARED]
    sends = [
        pltpu.make_async_copy(shared.at[pl.ds(at, to - at)], shared_hbm.at[pl.ds(at, to - at)], out_sem.at[i])
        for i, (at, to) in enumerate(zip(edges[:-1], edges[1:], strict=True))
    ]
    last, part = DECAY_AT - PIX, PIX // 8
    ends = [
        pltpu.make_async_copy(shared.at[pl.ds(last + i * part, part)], end_hbm.at[i], out_sem.at[len(sends) + i])
        for i in range(8)
    ]
    for copy in [small[0], *copies[:3], *frames[:group], *copies[3:], *frames[group:], small[1]]:
        copy.start()
    xpad[:, 0] = jnp.zeros((FRAMES, COLS, CIN), BF16)
    xpad[:, ROWS + 1] = jnp.zeros((FRAMES, COLS, CIN), BF16)
    small[0].wait()
    decay = decay_of(codes[...])
    shared[DECAY_AT:WEIGHT_AT] = jnp.broadcast_to(decay, (8, PD))
    running = jnp.zeros((PIX, PD), F32)
    for first in range(0, FRAMES, group):
        for copy in frames[first : first + group]:
            copy.wait()
        total = jnp.zeros((group * PIX, 3 * PD), F32)
        for di in range(3):
            if first == 0:
                for copy in copies[3 * di : 3 * di + 3]:
                    copy.wait()
            rows = xpad[first : first + group, di : di + ROWS].reshape(group * PIX, CIN)
            total = total + jnp.dot(rows, wcat[di], preferred_element_type=F32)
        drive = shifted_sum(total[:, :PD], total[:, PD : 2 * PD], total[:, 2 * PD :])
        for k in range(group):
            frame = first + k
            running = decay * running + drive[k * PIX : (k + 1) * PIX]
            shared[frame * PIX : (frame + 1) * PIX] = running
            if frame < FRAMES - 1:
                sends[frame].start()
        if first == 0:
            small[1].wait()
            for tap in range(9):
                for half in range(2):
                    at = WEIGHT_AT + (2 * tap + half) * PD
                    shared[at : at + PD] = wout[tap // 3, tap % 3, :, half * PD : (half + 1) * PD].astype(F32)
            sends[-1].start()
    for copy in ends:
        copy.start()
    sends[FRAMES - 1].start()
    for copy in ends + sends:
        copy.wait()


def total_kernel(ends_ref, codes_ref, out_ref):
    a8 = pow8(decay_of(codes_ref[...]))
    total = ends_ref[0]
    for z in range(1, 8):
        total = a8 * total + ends_ref[z]
    for y in range(8):
        out_ref[y] = total


def mix_kernel(own_ref, first_ref, second_ref, third_ref, out_ref):
    value = own_ref[...] + first_ref[...] + second_ref[...] + third_ref[...]
    half = 0.5 * value
    mixed = half + half * lax.erf(value * (0.5**0.5))
    out_ref[...] = mixed.astype(BF16)


def carry_kernel(ends_ref, totals_ref, codes_ref, wout_ref, other_ref, out_ref, w_ref):
    a8 = pow8(decay_of(codes_ref[...]))
    a64 = pow8(a8)
    own = lax.axis_index("y")
    carry = jnp.zeros((PIX // 8, PD), F32)
    for y in range(8):
        carry = jnp.where(y < own, a64 * carry + totals_ref[y], carry)
    for z in range(8):
        out_ref[z] = carry
        carry = a8 * carry + ends_ref[z]
    w_ref[:, :, :PD] = wout_ref[...]
    for tap in range(9):
        for half in range(2):
            at = WEIGHT_AT + (2 * tap + half) * PD
            w_ref[tap // 3, tap % 3, PD:, half * PD : (half + 1) * PD] = other_ref[at : at + PD].astype(BF16)


def readout(offset, own_ref, other_ref, codes_ref, carry_ref, carry_other_ref, w_ref, spad):
    chip = lax.axis_index("x") ^ (offset ^ (2 * (offset % 2) * lax.axis_index("c")))
    above = 4 * chip + 2 * lax.axis_index("c") - 1
    sides = (
        (own_ref, carry_ref, decay_of(codes_ref[...])),
        (other_ref, carry_other_ref, other_ref[DECAY_AT : DECAY_AT + 1]),
    )
    for row in range(4):
        inside = jnp.logical_and(above + row >= 0, above + row < ROWS)
        at = jnp.clip(above + row, 0, ROWS - 1)
        for side, (ref, carried, decay) in enumerate(sides):
            half = pl.ds(pl.multiple_of(at % 2 * COLS, COLS), COLS)
            carry = jnp.where(inside, carried[at // 2, half], 0.0)
            for j in range(FRAMES):
                carry = decay * carry
                state = ref[pl.ds(pl.multiple_of(at * COLS + j * PIX, COLS), COLS)]
                state = jnp.where(inside, state, 0.0) + carry
                spad[j, row, :, side * PD : (side + 1) * PD] = state.astype(BF16)
    rows = [spad[:, di : di + 2].reshape(FRAMES * 2 * COLS, 2 * PD) for di in range(3)]
    taps = []
    for dj in range(3):
        total = jnp.dot(rows[0], w_ref[0, dj], preferred_element_type=F32)
        for di in range(1, 3):
            total = total + jnp.dot(rows[di], w_ref[di, dj], preferred_element_type=F32)
        taps.append(total)
    return shifted_sum(*taps)


def far_kernel(offset, own_ref, other_ref, codes_ref, carry_ref, carry_other_ref, w_ref, after_ref, out_ref, spad):
    out_ref[...] = readout(offset, own_ref, other_ref, codes_ref, carry_ref, carry_other_ref, w_ref, spad)


def near_kernel(own_ref, other_ref, codes_ref, carry_ref, carry_other_ref, w_ref, after_ref, x_hbm, gain_ref,
                out_ref, spad, frames, sem):
    start = 4 * lax.axis_index("x") + 2 * lax.axis_index("c")
    copy = pltpu.make_async_copy(x_hbm.at[:, pl.ds(start, 2)], frames, sem)
    copy.start()
    value = readout(0, own_ref, other_ref, codes_ref, carry_ref, carry_other_ref, w_ref, spad)
    copy.wait()
    out_ref[...] = value + frames[...].reshape(FRAMES * 2 * COLS, CIN).astype(F32) * gain_ref[...]


def call(kernel, out, args, spaces=None, scratch=(), flops=0, moved=1 << 20, limit=24, outs=None):
    return pl.pallas_call(
        kernel,
        out_shape=out,
        in_specs=[pl.BlockSpec(memory_space=space) for space in spaces or [pltpu.VMEM] * len(args)],
        out_specs=outs or jax.tree.map(lambda _: pl.BlockSpec(memory_space=pltpu.VMEM), out),
        scratch_shapes=list(scratch),
        compiler_params=pltpu.CompilerParams(vmem_limit_bytes=limit << 20),
        cost_estimate=pl.CostEstimate(flops=flops, bytes_accessed=moved, transcendentals=0),
    )(*args)


def swaps(offset):
    return [(2 * x + c, 2 * (x ^ offset ^ (2 * (offset % 2) * c)) + c) for x in range(4) for c in range(2)]


def shape(*dims, dtype=F32):
    return jax.ShapeDtypeStruct(dims, dtype)


def per_device(frames, in_weight, decay_codes, out_weight, skip_gain):
    codes = decay_codes.reshape(1, PD)
    flops = 2 * FRAMES * PIX * 9 * CIN * PD
    slices = shape(8, PIX // 8, PD)
    owned = FRAMES * 2 * COLS
    shared, end = call(
        drive_kernel,
        (shape(SHARED, PD), slices),
        (frames, in_weight, codes, out_weight),
        spaces=[pltpu.HBM] * 4,
        scratch=(
            pltpu.VMEM((FRAMES, ROWS + 2, COLS, CIN), BF16),
            pltpu.VMEM((3, CIN, 3 * PD), BF16),
            pltpu.VMEM((3, 3, PD, CIN), BF16),
            pltpu.VMEM((1, PD), jnp.int32),
            pltpu.VMEM((SHARED, PD), F32),
            pltpu.SemaphoreType.DMA((FRAMES,)),
            pltpu.SemaphoreType.DMA((9,)),
            pltpu.SemaphoreType.DMA((2,)),
            pltpu.SemaphoreType.DMA((17,)),
        ),
        flops=flops,
        moved=3 << 20,
        limit=59,
        outs=tuple(pl.BlockSpec(memory_space=space) for space in (pltpu.HBM, pltpu.HBM)),
    )
    swap = [(0, 1), (1, 0)]
    ends = lax.all_to_all(end, "z", 0, 0, tiled=True)
    other = lax.ppermute(shared, "c", swap)
    total = call(total_kernel, slices, (ends, codes))
    totals = lax.all_to_all(total, "y", 0, 0, tiled=True)
    carries, weights = call(
        carry_kernel,
        (slices, shape(3, 3, 2 * PD, CIN, dtype=BF16)),
        (ends, totals, codes, out_weight, other),
    )
    carry = lax.all_to_all(carries, "z", 0, 0, tiled=True)
    carry_other = lax.ppermute(carry, "c", swap)
    inputs = (shared, other, codes, carry, carry_other, weights)
    padded = pltpu.VMEM((FRAMES, 4, COLS, 2 * PD), BF16)
    piece, arrived = carry_other, []
    for offset in ORDER:
        piece = call(
            functools.partial(far_kernel, offset),
            shape(owned, CIN),
            (*inputs, piece),
            spaces=[pltpu.VMEM] * 6 + [pl.ANY],
            scratch=(padded,),
            flops=flops // 4,
        )
        arrived.append(lax.ppermute(piece, ("x", "c"), swaps(offset)))
    own = call(
        near_kernel,
        shape(owned, CIN),
        (*inputs, piece, frames, skip_gain.reshape(1, CIN)),
        spaces=[pltpu.VMEM] * 6 + [pl.ANY, pltpu.HBM, pltpu.VMEM],
        scratch=(padded, pltpu.VMEM((FRAMES, 2, COLS, CIN), BF16), pltpu.SemaphoreType.DMA),
        flops=flops // 4,
    )
    mixed = call(mix_kernel, shape(owned, CIN, dtype=BF16), (own, *arrived))
    return mixed.reshape(FRAMES, 2, COLS, CIN)


def solution(mesh):
    finer = Mesh(mesh.devices.reshape(8, 8, 4, 2), ("y", "z", "x", "c"))
    chan = ("x", "c")
    placed = (
        P(("y", "z"), None, None, None),
        P(None, None, None, chan),
        P(chan),
        P(None, None, chan, None),
        P(),
    )
    return jax.shard_map(
        per_device,
        mesh=finer,
        in_specs=placed,
        out_specs=P(("y", "z"), chan, None, None),
        check_vma=False,
    )
```

```python
import functools


import jax
import jax.numpy as jnp
from jax import lax
from jax.experimental import pallas as pl
from jax.experimental.pallas import tpu as pltpu
from jax.sharding import Mesh
from jax.sharding import PartitionSpec as P

FRAMES, ROWS, COLS, CIN, PD = 8, 16, 16, 256, 128
PIX = ROWS * COLS
DECAY_AT = FRAMES * PIX
WEIGHT_AT = DECAY_AT + 8
SHARED = WEIGHT_AT + 18 * PD
OPPOSITE, FIRST, LAST = 2, 1, 3
F32, BF16 = jnp.float32, jnp.bfloat16


def decay_of(codes):
    return 1.0 - codes.astype(F32) / 4096.0


def pow8(value):
    value = value * value
    value = value * value
    return value * value


def shifted_sum(left, centre, right):
    count = left.shape[0]
    column = lax.broadcasted_iota(jnp.int32, left.shape, 0) % COLS
    from_left = jnp.where(column == 0, 0.0, pltpu.roll(left, 1, 0))
    from_right = jnp.where(column == COLS - 1, 0.0, pltpu.roll(right, count - 1, 0))
    return from_left + centre + from_right


def drive_kernel(x_hbm, w_hbm, codes_hbm, wout_hbm, shared_hbm, end_hbm,
                 xpad, wcat, wout, codes, shared, frame_sem, tap_sem, small_sem, out_sem):
    taps = [(di, dj) for di in range(3) for dj in range(3)]
    copies = [
        pltpu.make_async_copy(w_hbm.at[di, dj], wcat.at[di, :, pl.ds(dj * PD, PD)], tap_sem.at[3 * di + dj])
        for di, dj in taps
    ]
    frames = [
        pltpu.make_async_copy(x_hbm.at[j], xpad.at[j, pl.ds(1, ROWS)], frame_sem.at[j]) for j in range(FRAMES)
    ]
    small = [
        pltpu.make_async_copy(src, dst, small_sem.at[i])
        for i, (src, dst) in enumerate(((codes_hbm, codes), (wout_hbm, wout)))
    ]
    group = FRAMES // 2
    edges = [*range(0, DECAY_AT, PIX), DECAY_AT, SHARED]
    sends = [
        pltpu.make_async_copy(shared.at[pl.ds(at, to - at)], shared_hbm.at[pl.ds(at, to - at)], out_sem.at[i])
        for i, (at, to) in enumerate(zip(edges[:-1], edges[1:], strict=True))
    ]
    last, part = DECAY_AT - PIX, PIX // 8
    ends = [
        pltpu.make_async_copy(shared.at[pl.ds(last + i * part, part)], end_hbm.at[i], out_sem.at[len(sends) + i])
        for i in range(8)
    ]
    for copy in [small[0], *copies[:3], *frames[:group], *copies[3:], *frames[group:], small[1]]:
        copy.start()
    xpad[:, 0] = jnp.zeros((FRAMES, COLS, CIN), BF16)
    xpad[:, ROWS + 1] = jnp.zeros((FRAMES, COLS, CIN), BF16)
    small[0].wait()
    decay = decay_of(codes[...])
    shared[DECAY_AT:WEIGHT_AT] = jnp.broadcast_to(decay, (8, PD))
    running = jnp.zeros((PIX, PD), F32)
    for first in range(0, FRAMES, group):
        for copy in frames[first : first + group]:
            copy.wait()
        total = jnp.zeros((group * PIX, 3 * PD), F32)
        for di in range(3):
            if first == 0:
                for copy in copies[3 * di : 3 * di + 3]:
                    copy.wait()
            rows = xpad[first : first + group, di : di + ROWS].reshape(group * PIX, CIN)
            total = total + jnp.dot(rows, wcat[di], preferred_element_type=F32)
        drive = shifted_sum(total[:, :PD], total[:, PD : 2 * PD], total[:, 2 * PD :])
        for k in range(group):
            frame = first + k
            running = decay * running + drive[k * PIX : (k + 1) * PIX]
            shared[frame * PIX : (frame + 1) * PIX] = running
            if frame < FRAMES - 1:
                sends[frame].start()
        if first == 0:
            small[1].wait()
            for tap in range(9):
                for half in range(2):
                    at = WEIGHT_AT + (2 * tap + half) * PD
                    shared[at : at + PD] = wout[tap // 3, tap % 3, :, half * PD : (half + 1) * PD].astype(F32)
            sends[-1].start()
    for copy in ends:
        copy.start()
    sends[FRAMES - 1].start()
    for copy in ends + sends:
        copy.wait()


def total_kernel(ends_ref, codes_ref, out_ref):
    a8 = pow8(decay_of(codes_ref[...]))
    total = ends_ref[0]
    for z in range(1, 8):
        total = a8 * total + ends_ref[z]
    for y in range(8):
        out_ref[y] = total


def mix_kernel(own_ref, first_ref, last_ref, out_ref):
    value = own_ref[...] + first_ref[...] + last_ref[...]
    half = 0.5 * value
    mixed = half + half * lax.erf(value * (0.5**0.5))
    out_ref[...] = mixed.astype(BF16)


def carry_kernel(ends_ref, totals_ref, codes_ref, wout_ref, other_ref, out_ref, w_ref):
    a8 = pow8(decay_of(codes_ref[...]))
    a64 = pow8(a8)
    own = lax.axis_index("y")
    carry = jnp.zeros((PIX // 8, PD), F32)
    for y in range(8):
        carry = jnp.where(y < own, a64 * carry + totals_ref[y], carry)
    for z in range(8):
        out_ref[z] = carry
        carry = a8 * carry + ends_ref[z]
    w_ref[:, :, :PD] = wout_ref[...]
    for tap in range(9):
        for half in range(2):
            at = WEIGHT_AT + (2 * tap + half) * PD
            w_ref[tap // 3, tap % 3, PD:, half * PD : (half + 1) * PD] = other_ref[at : at + PD].astype(BF16)


def readout(offset, own_ref, other_ref, codes_ref, carry_ref, carry_other_ref, w_ref, spad):
    chip = lax.axis_index("x") ^ (offset ^ (2 * (offset % 2) * lax.axis_index("c")))
    above = 4 * chip + 2 * lax.axis_index("c") - 1
    sides = (
        (own_ref, carry_ref, decay_of(codes_ref[...])),
        (other_ref, carry_other_ref, other_ref[DECAY_AT : DECAY_AT + 1]),
    )
    for row in range(4):
        inside = jnp.logical_and(above + row >= 0, above + row < ROWS)
        at = jnp.clip(above + row, 0, ROWS - 1)
        for side, (ref, carried, decay) in enumerate(sides):
            half = pl.ds(pl.multiple_of(at % 2 * COLS, COLS), COLS)
            carry = jnp.where(inside, carried[at // 2, half], 0.0)
            for j in range(FRAMES):
                carry = decay * carry
                state = ref[pl.ds(pl.multiple_of(at * COLS + j * PIX, COLS), COLS)]
                state = jnp.where(inside, state, 0.0) + carry
                spad[j, row, :, side * PD : (side + 1) * PD] = state.astype(BF16)
    rows = [spad[:, di : di + 2].reshape(FRAMES * 2 * COLS, 2 * PD) for di in range(3)]
    taps = []
    for dj in range(3):
        total = jnp.dot(rows[0], w_ref[0, dj], preferred_element_type=F32)
        for di in range(1, 3):
            total = total + jnp.dot(rows[di], w_ref[di, dj], preferred_element_type=F32)
        taps.append(total)
    return shifted_sum(*taps)


def far_kernel(offset, own_ref, other_ref, codes_ref, carry_ref, carry_other_ref, w_ref, after_ref, out_ref, spad):
    value = readout(offset, own_ref, other_ref, codes_ref, carry_ref, carry_other_ref, w_ref, spad)
    if offset == LAST:
        value = value + after_ref[...]
    out_ref[...] = value


def near_kernel(own_ref, other_ref, codes_ref, carry_ref, carry_other_ref, w_ref, after_ref, x_hbm, gain_ref,
                out_ref, spad, frames, sem):
    start = 4 * lax.axis_index("x") + 2 * lax.axis_index("c")
    copy = pltpu.make_async_copy(x_hbm.at[:, pl.ds(start, 2)], frames, sem)
    copy.start()
    value = readout(0, own_ref, other_ref, codes_ref, carry_ref, carry_other_ref, w_ref, spad)
    copy.wait()
    out_ref[...] = value + frames[...].reshape(FRAMES * 2 * COLS, CIN).astype(F32) * gain_ref[...]


def call(kernel, out, args, spaces=None, scratch=(), flops=0, moved=1 << 20, limit=24, outs=None):
    return pl.pallas_call(
        kernel,
        out_shape=out,
        in_specs=[pl.BlockSpec(memory_space=space) for space in spaces or [pltpu.VMEM] * len(args)],
        out_specs=outs or jax.tree.map(lambda _: pl.BlockSpec(memory_space=pltpu.VMEM), out),
        scratch_shapes=list(scratch),
        compiler_params=pltpu.CompilerParams(vmem_limit_bytes=limit << 20),
        cost_estimate=pl.CostEstimate(flops=flops, bytes_accessed=moved, transcendentals=0),
    )(*args)


def swaps(offset):
    return [(2 * x + c, 2 * (x ^ offset ^ (2 * (offset % 2) * c)) + c) for x in range(4) for c in range(2)]


def shape(*dims, dtype=F32):
    return jax.ShapeDtypeStruct(dims, dtype)


def per_device(frames, in_weight, decay_codes, out_weight, skip_gain):
    codes = decay_codes.reshape(1, PD)
    flops = 2 * FRAMES * PIX * 9 * CIN * PD
    slices = shape(8, PIX // 8, PD)
    owned = FRAMES * 2 * COLS
    shared, end = call(
        drive_kernel,
        (shape(SHARED, PD), slices),
        (frames, in_weight, codes, out_weight),
        spaces=[pltpu.HBM] * 4,
        scratch=(
            pltpu.VMEM((FRAMES, ROWS + 2, COLS, CIN), BF16),
            pltpu.VMEM((3, CIN, 3 * PD), BF16),
            pltpu.VMEM((3, 3, PD, CIN), BF16),
            pltpu.VMEM((1, PD), jnp.int32),
            pltpu.VMEM((SHARED, PD), F32),
            pltpu.SemaphoreType.DMA((FRAMES,)),
            pltpu.SemaphoreType.DMA((9,)),
            pltpu.SemaphoreType.DMA((2,)),
            pltpu.SemaphoreType.DMA((17,)),
        ),
        flops=flops,
        moved=3 << 20,
        limit=59,
        outs=tuple(pl.BlockSpec(memory_space=space) for space in (pltpu.HBM, pltpu.HBM)),
    )
    swap = [(0, 1), (1, 0)]
    ends = lax.all_to_all(end, "z", 0, 0, tiled=True)
    other = lax.ppermute(shared, "c", swap)
    total = call(total_kernel, slices, (ends, codes))
    totals = lax.all_to_all(total, "y", 0, 0, tiled=True)
    carries, weights = call(
        carry_kernel,
        (slices, shape(3, 3, 2 * PD, CIN, dtype=BF16)),
        (ends, totals, codes, out_weight, other),
    )
    carry = lax.all_to_all(carries, "z", 0, 0, tiled=True)
    carry_other = lax.ppermute(carry, "c", swap)
    inputs = (shared, other, codes, carry, carry_other, weights)
    padded = pltpu.VMEM((FRAMES, 4, COLS, 2 * PD), BF16)

    def far(offset, after, space):
        return call(
            functools.partial(far_kernel, offset),
            shape(owned, CIN),
            (*inputs, after),
            spaces=[pltpu.VMEM] * 6 + [space],
            scratch=(padded,),
            flops=flops // 4,
        )

    def send(piece, to):
        return lax.ppermute(piece, ("x", "c"), swaps(to))

    opposite = far(OPPOSITE, carry_other, pl.ANY)
    relayed = send(opposite, FIRST)
    piece = far(FIRST, opposite, pl.ANY)
    first = send(piece, FIRST)
    piece = far(LAST, relayed, pltpu.VMEM)
    last = send(piece, LAST)
    own = call(
        near_kernel,
        shape(owned, CIN),
        (*inputs, piece, frames, skip_gain.reshape(1, CIN)),
        spaces=[pltpu.VMEM] * 6 + [pl.ANY, pltpu.HBM, pltpu.VMEM],
        scratch=(padded, pltpu.VMEM((FRAMES, 2, COLS, CIN), BF16), pltpu.SemaphoreType.DMA),
        flops=flops // 4,
    )
    mixed = call(mix_kernel, shape(owned, CIN, dtype=BF16), (own, first, last))
    return mixed.reshape(FRAMES, 2, COLS, CIN)


def solution(mesh):
    finer = Mesh(mesh.devices.reshape(8, 8, 4, 2), ("y", "z", "x", "c"))
    chan = ("x", "c")
    placed = (
        P(("y", "z"), None, None, None),
        P(None, None, None, chan),
        P(chan),
        P(None, None, chan, None),
        P(),
    )
    return jax.shard_map(
        per_device,
        mesh=finer,
        in_specs=placed,
        out_specs=P(("y", "z"), chan, None, None),
        check_vma=False,
    )
```

```python
import functools


import jax
import jax.numpy as jnp
from jax import lax
from jax.experimental import pallas as pl
from jax.experimental.pallas import tpu as pltpu
from jax.sharding import Mesh
from jax.sharding import PartitionSpec as P

FRAMES, ROWS, COLS, CIN, PD = 8, 16, 16, 256, 128
PIX = ROWS * COLS
DECAY_AT = FRAMES * PIX
WEIGHT_AT = DECAY_AT + 8
SHARED = WEIGHT_AT + 18 * PD
OPPOSITE, FIRST, LAST = 2, 1, 3
F32, BF16 = jnp.float32, jnp.bfloat16


def decay_of(codes):
    return 1.0 - codes.astype(F32) / 4096.0


def pow8(value):
    value = value * value
    value = value * value
    return value * value


def shifted_sum(left, centre, right):
    count = left.shape[0]
    column = lax.broadcasted_iota(jnp.int32, left.shape, 0) % COLS
    from_left = jnp.where(column == 0, 0.0, pltpu.roll(left, 1, 0))
    from_right = jnp.where(column == COLS - 1, 0.0, pltpu.roll(right, count - 1, 0))
    return from_left + centre + from_right


def drive_kernel(x_hbm, w_hbm, codes_hbm, wout_hbm, shared_hbm, end_hbm,
                 xpad, wcat, wout, codes, shared, frame_sem, tap_sem, small_sem, out_sem):
    taps = [(di, dj) for di in range(3) for dj in range(3)]
    copies = [
        pltpu.make_async_copy(w_hbm.at[di, dj], wcat.at[di, :, pl.ds(dj * PD, PD)], tap_sem.at[3 * di + dj])
        for di, dj in taps
    ]
    frames = [
        pltpu.make_async_copy(x_hbm.at[j], xpad.at[j, pl.ds(1, ROWS)], frame_sem.at[j]) for j in range(FRAMES)
    ]
    small = [
        pltpu.make_async_copy(src, dst, small_sem.at[i])
        for i, (src, dst) in enumerate(((codes_hbm, codes), (wout_hbm, wout)))
    ]
    group = FRAMES // 2
    edges = [*range(0, DECAY_AT, PIX), DECAY_AT, SHARED]
    sends = [
        pltpu.make_async_copy(shared.at[pl.ds(at, to - at)], shared_hbm.at[pl.ds(at, to - at)], out_sem.at[i])
        for i, (at, to) in enumerate(zip(edges[:-1], edges[1:], strict=True))
    ]
    last, part = DECAY_AT - PIX, PIX // 8
    ends = [
        pltpu.make_async_copy(shared.at[pl.ds(last + i * part, part)], end_hbm.at[i], out_sem.at[len(sends) + i])
        for i in range(8)
    ]
    for copy in [small[0], *copies[:3], *frames[:group], *copies[3:], *frames[group:], small[1]]:
        copy.start()
    xpad[:, 0] = jnp.zeros((FRAMES, COLS, CIN), BF16)
    xpad[:, ROWS + 1] = jnp.zeros((FRAMES, COLS, CIN), BF16)
    small[0].wait()
    decay = decay_of(codes[...])
    shared[DECAY_AT:WEIGHT_AT] = jnp.broadcast_to(decay, (8, PD))
    running = jnp.zeros((PIX, PD), F32)
    for first in range(0, FRAMES, group):
        for copy in frames[first : first + group]:
            copy.wait()
        total = jnp.zeros((group * PIX, 3 * PD), F32)
        for di in range(3):
            if first == 0:
                for copy in copies[3 * di : 3 * di + 3]:
                    copy.wait()
            rows = xpad[first : first + group, di : di + ROWS].reshape(group * PIX, CIN)
            total = total + jnp.dot(rows, wcat[di], preferred_element_type=F32)
        drive = shifted_sum(total[:, :PD], total[:, PD : 2 * PD], total[:, 2 * PD :])
        for k in range(group):
            frame = first + k
            running = decay * running + drive[k * PIX : (k + 1) * PIX]
            shared[frame * PIX : (frame + 1) * PIX] = running
            if frame < FRAMES - 1:
                sends[frame].start()
        if first == 0:
            small[1].wait()
            for tap in range(9):
                for half in range(2):
                    at = WEIGHT_AT + (2 * tap + half) * PD
                    shared[at : at + PD] = wout[tap // 3, tap % 3, :, half * PD : (half + 1) * PD].astype(F32)
            sends[-1].start()
    for copy in ends:
        copy.start()
    sends[FRAMES - 1].start()
    for copy in ends + sends:
        copy.wait()


def total_kernel(ends_ref, codes_ref, out_ref):
    a8 = pow8(decay_of(codes_ref[...]))
    total = ends_ref[0]
    for z in range(1, 8):
        total = a8 * total + ends_ref[z]
    for y in range(8):
        out_ref[y] = total


def mix_kernel(own_ref, first_ref, last_ref, out_ref):
    value = own_ref[...] + first_ref[...] + last_ref[...]
    half = 0.5 * value
    mixed = half + half * lax.erf(value * (0.5**0.5))
    out_ref[...] = mixed.astype(BF16)


def carry_kernel(ends_ref, totals_ref, codes_ref, wout_ref, other_ref, out_ref, w_ref):
    a8 = pow8(decay_of(codes_ref[...]))
    a64 = pow8(a8)
    own = lax.axis_index("y")
    carry = jnp.zeros((PIX // 8, PD), F32)
    for y in range(8):
        carry = jnp.where(y < own, a64 * carry + totals_ref[y], carry)
    for z in range(8):
        out_ref[z] = carry
        carry = a8 * carry + ends_ref[z]
    w_ref[:, :, :PD] = wout_ref[...]
    for tap in range(9):
        for half in range(2):
            at = WEIGHT_AT + (2 * tap + half) * PD
            w_ref[tap // 3, tap % 3, PD:, half * PD : (half + 1) * PD] = other_ref[at : at + PD].astype(BF16)


def readout(offset, own_ref, other_ref, codes_ref, carry_ref, carry_other_ref, w_ref, spad):
    chip = lax.axis_index("x") ^ (offset ^ (2 * (offset % 2) * (1 - lax.axis_index("c"))))
    above = 4 * chip + 2 * lax.axis_index("c") - 1
    sides = (
        (own_ref, carry_ref, decay_of(codes_ref[...])),
        (other_ref, carry_other_ref, other_ref[DECAY_AT : DECAY_AT + 1]),
    )
    for row in range(4):
        inside = jnp.logical_and(above + row >= 0, above + row < ROWS)
        at = jnp.clip(above + row, 0, ROWS - 1)
        for side, (ref, carried, decay) in enumerate(sides):
            half = pl.ds(pl.multiple_of(at % 2 * COLS, COLS), COLS)
            carry = jnp.where(inside, carried[at // 2, half], 0.0)
            for j in range(FRAMES):
                carry = decay * carry
                state = ref[pl.ds(pl.multiple_of(at * COLS + j * PIX, COLS), COLS)]
                state = jnp.where(inside, state, 0.0) + carry
                spad[j, row, :, side * PD : (side + 1) * PD] = state.astype(BF16)
    rows = [spad[:, di : di + 2].reshape(FRAMES * 2 * COLS, 2 * PD) for di in range(3)]
    taps = []
    for dj in range(3):
        total = jnp.dot(rows[0], w_ref[0, dj], preferred_element_type=F32)
        for di in range(1, 3):
            total = total + jnp.dot(rows[di], w_ref[di, dj], preferred_element_type=F32)
        taps.append(total)
    return shifted_sum(*taps)


def far_kernel(offset, own_ref, other_ref, codes_ref, carry_ref, carry_other_ref, w_ref, after_ref, out_ref, spad):
    out_ref[...] = readout(offset, own_ref, other_ref, codes_ref, carry_ref, carry_other_ref, w_ref, spad)


def join_kernel(piece_ref, relayed_ref, after_ref, out_ref):
    out_ref[...] = piece_ref[...] + relayed_ref[...]


def near_kernel(own_ref, other_ref, codes_ref, carry_ref, carry_other_ref, w_ref, after_ref, x_hbm, gain_ref,
                out_ref, spad, frames, sem):
    start = 4 * lax.axis_index("x") + 2 * lax.axis_index("c")
    copy = pltpu.make_async_copy(x_hbm.at[:, pl.ds(start, 2)], frames, sem)
    copy.start()
    value = readout(0, own_ref, other_ref, codes_ref, carry_ref, carry_other_ref, w_ref, spad)
    copy.wait()
    out_ref[...] = value + frames[...].reshape(FRAMES * 2 * COLS, CIN).astype(F32) * gain_ref[...]


def call(kernel, out, args, spaces=None, scratch=(), flops=0, moved=1 << 20, limit=24, outs=None):
    return pl.pallas_call(
        kernel,
        out_shape=out,
        in_specs=[pl.BlockSpec(memory_space=space) for space in spaces or [pltpu.VMEM] * len(args)],
        out_specs=outs or jax.tree.map(lambda _: pl.BlockSpec(memory_space=pltpu.VMEM), out),
        scratch_shapes=list(scratch),
        compiler_params=pltpu.CompilerParams(vmem_limit_bytes=limit << 20),
        cost_estimate=pl.CostEstimate(flops=flops, bytes_accessed=moved, transcendentals=0),
    )(*args)


def swaps(offset):
    return [(2 * x + c, 2 * (x ^ offset ^ (2 * (offset % 2) * (1 - c))) + c) for x in range(4) for c in range(2)]


def shape(*dims, dtype=F32):
    return jax.ShapeDtypeStruct(dims, dtype)


def per_device(frames, in_weight, decay_codes, out_weight, skip_gain):
    codes = decay_codes.reshape(1, PD)
    flops = 2 * FRAMES * PIX * 9 * CIN * PD
    slices = shape(8, PIX // 8, PD)
    owned = FRAMES * 2 * COLS
    shared, end = call(
        drive_kernel,
        (shape(SHARED, PD), slices),
        (frames, in_weight, codes, out_weight),
        spaces=[pltpu.HBM] * 4,
        scratch=(
            pltpu.VMEM((FRAMES, ROWS + 2, COLS, CIN), BF16),
            pltpu.VMEM((3, CIN, 3 * PD), BF16),
            pltpu.VMEM((3, 3, PD, CIN), BF16),
            pltpu.VMEM((1, PD), jnp.int32),
            pltpu.VMEM((SHARED, PD), F32),
            pltpu.SemaphoreType.DMA((FRAMES,)),
            pltpu.SemaphoreType.DMA((9,)),
            pltpu.SemaphoreType.DMA((2,)),
            pltpu.SemaphoreType.DMA((17,)),
        ),
        flops=flops,
        moved=3 << 20,
        limit=59,
        outs=tuple(pl.BlockSpec(memory_space=space) for space in (pltpu.HBM, pltpu.HBM)),
    )
    swap = [(0, 1), (1, 0)]
    ends = lax.all_to_all(end, "z", 0, 0, tiled=True)
    other = lax.ppermute(shared, "c", swap)
    total = call(total_kernel, slices, (ends, codes))
    totals = lax.all_to_all(total, "y", 0, 0, tiled=True)
    carries, weights = call(
        carry_kernel,
        (slices, shape(3, 3, 2 * PD, CIN, dtype=BF16)),
        (ends, totals, codes, out_weight, other),
    )
    carry = lax.all_to_all(carries, "z", 0, 0, tiled=True)
    carry_other = lax.ppermute(carry, "c", swap)
    inputs = (shared, other, codes, carry, carry_other, weights)
    padded = pltpu.VMEM((FRAMES, 4, COLS, 2 * PD), BF16)

    def far(offset, after):
        return call(
            functools.partial(far_kernel, offset),
            shape(owned, CIN),
            (*inputs, after),
            spaces=[pltpu.VMEM] * 6 + [pl.ANY],
            scratch=(padded,),
            flops=flops // 4,
        )

    def send(piece, to):
        return lax.ppermute(piece, ("x", "c"), swaps(to))

    opposite = far(OPPOSITE, carry_other)
    relayed = send(opposite, FIRST)
    piece = far(FIRST, opposite)
    first = send(piece, FIRST)
    piece = far(LAST, piece)
    own = call(
        near_kernel,
        shape(owned, CIN),
        (*inputs, piece, frames, skip_gain.reshape(1, CIN)),
        spaces=[pltpu.VMEM] * 6 + [pl.ANY, pltpu.HBM, pltpu.VMEM],
        scratch=(padded, pltpu.VMEM((FRAMES, 2, COLS, CIN), BF16), pltpu.SemaphoreType.DMA),
        flops=flops // 4,
    )
    piece = call(
        join_kernel, shape(owned, CIN), (piece, relayed, own), spaces=[pltpu.VMEM] * 2 + [pl.ANY]
    )
    last = send(piece, LAST)
    mixed = call(mix_kernel, shape(owned, CIN, dtype=BF16), (own, first, last))
    return mixed.reshape(FRAMES, 2, COLS, CIN)


def solution(mesh):
    finer = Mesh(mesh.devices.reshape(8, 8, 4, 2), ("y", "z", "x", "c"))
    chan = ("x", "c")
    placed = (
        P(("y", "z"), None, None, None),
        P(None, None, None, chan),
        P(chan),
        P(None, None, chan, None),
        P(),
    )
    return jax.shard_map(
        per_device,
        mesh=finer,
        in_specs=placed,
        out_specs=P(("y", "z"), chan, None, None),
        check_vma=False,
    )
```

```python
import functools


import jax
import jax.numpy as jnp
from jax import lax
from jax.experimental import pallas as pl
from jax.experimental.pallas import tpu as pltpu
from jax.sharding import Mesh
from jax.sharding import PartitionSpec as P

FRAMES, ROWS, COLS, CIN, PD = 8, 16, 16, 256, 128
PIX = ROWS * COLS
DECAY_AT = FRAMES * PIX
WEIGHT_AT = DECAY_AT + 8
SHARED = WEIGHT_AT + 18 * PD
OPPOSITE, FIRST, LAST = 2, 1, 3
F32, BF16 = jnp.float32, jnp.bfloat16


def decay_of(codes):
    return 1.0 - codes.astype(F32) / 4096.0


def pow8(value):
    value = value * value
    value = value * value
    return value * value


def shifted_sum(left, centre, right):
    count = left.shape[0]
    column = lax.broadcasted_iota(jnp.int32, left.shape, 0) % COLS
    from_left = jnp.where(column == 0, 0.0, pltpu.roll(left, 1, 0))
    from_right = jnp.where(column == COLS - 1, 0.0, pltpu.roll(right, count - 1, 0))
    return from_left + centre + from_right


def drive_kernel(x_hbm, w_hbm, codes_hbm, wout_hbm, shared_hbm, end_hbm,
                 xpad, wcat, wout, codes, shared, frame_sem, tap_sem, small_sem, out_sem):
    taps = [(di, dj) for di in range(3) for dj in range(3)]
    copies = [
        pltpu.make_async_copy(w_hbm.at[di, dj], wcat.at[di, :, pl.ds(dj * PD, PD)], tap_sem.at[3 * di + dj])
        for di, dj in taps
    ]
    frames = [
        pltpu.make_async_copy(x_hbm.at[j], xpad.at[j, pl.ds(1, ROWS)], frame_sem.at[j]) for j in range(FRAMES)
    ]
    small = [
        pltpu.make_async_copy(src, dst, small_sem.at[i])
        for i, (src, dst) in enumerate(((codes_hbm, codes), (wout_hbm, wout)))
    ]
    group = FRAMES // 2
    edges = [*range(0, DECAY_AT, PIX), DECAY_AT, SHARED]
    sends = [
        pltpu.make_async_copy(shared.at[pl.ds(at, to - at)], shared_hbm.at[pl.ds(at, to - at)], out_sem.at[i])
        for i, (at, to) in enumerate(zip(edges[:-1], edges[1:], strict=True))
    ]
    last, part = DECAY_AT - PIX, PIX // 8
    ends = [
        pltpu.make_async_copy(shared.at[pl.ds(last + i * part, part)], end_hbm.at[i], out_sem.at[len(sends) + i])
        for i in range(8)
    ]
    for copy in [small[0], *copies[:3], *frames[:group], *copies[3:], *frames[group:], small[1]]:
        copy.start()
    xpad[:, 0] = jnp.zeros((FRAMES, COLS, CIN), BF16)
    xpad[:, ROWS + 1] = jnp.zeros((FRAMES, COLS, CIN), BF16)
    small[0].wait()
    decay = decay_of(codes[...])
    shared[DECAY_AT:WEIGHT_AT] = jnp.broadcast_to(decay, (8, PD))
    running = jnp.zeros((PIX, PD), F32)
    for first in range(0, FRAMES, group):
        for copy in frames[first : first + group]:
            copy.wait()
        total = jnp.zeros((group * PIX, 3 * PD), F32)
        for di in range(3):
            if first == 0:
                for copy in copies[3 * di : 3 * di + 3]:
                    copy.wait()
            rows = xpad[first : first + group, di : di + ROWS].reshape(group * PIX, CIN)
            total = total + jnp.dot(rows, wcat[di], preferred_element_type=F32)
        drive = shifted_sum(total[:, :PD], total[:, PD : 2 * PD], total[:, 2 * PD :])
        for k in range(group):
            frame = first + k
            running = decay * running + drive[k * PIX : (k + 1) * PIX]
            shared[frame * PIX : (frame + 1) * PIX] = running
            if frame < FRAMES - 1:
                sends[frame].start()
        if first == 0:
            small[1].wait()
            for tap in range(9):
                for half in range(2):
                    at = WEIGHT_AT + (2 * tap + half) * PD
                    shared[at : at + PD] = wout[tap // 3, tap % 3, :, half * PD : (half + 1) * PD].astype(F32)
            sends[-1].start()
    for copy in ends:
        copy.start()
    sends[FRAMES - 1].start()
    for copy in ends + sends:
        copy.wait()


def total_kernel(ends_ref, codes_ref, out_ref):
    a8 = pow8(decay_of(codes_ref[...]))
    total = ends_ref[0]
    for z in range(1, 8):
        total = a8 * total + ends_ref[z]
    for y in range(8):
        out_ref[y] = total


def mix_kernel(ready_ref, last_ref, out_ref):
    value = ready_ref[...] + last_ref[...]
    half = 0.5 * value
    mixed = half + half * lax.erf(value * (0.5**0.5))
    out_ref[...] = mixed.astype(BF16)


def carry_kernel(ends_ref, totals_ref, codes_ref, wout_ref, other_ref, out_ref, w_ref):
    a8 = pow8(decay_of(codes_ref[...]))
    a64 = pow8(a8)
    own = lax.axis_index("y")
    carry = jnp.zeros((PIX // 8, PD), F32)
    for y in range(8):
        carry = jnp.where(y < own, a64 * carry + totals_ref[y], carry)
    for z in range(8):
        out_ref[z] = carry
        carry = a8 * carry + ends_ref[z]
    w_ref[:, :, :PD] = wout_ref[...]
    for tap in range(9):
        for half in range(2):
            at = WEIGHT_AT + (2 * tap + half) * PD
            w_ref[tap // 3, tap % 3, PD:, half * PD : (half + 1) * PD] = other_ref[at : at + PD].astype(BF16)


def readout(offset, own_ref, other_ref, codes_ref, carry_ref, carry_other_ref, w_ref, spad):
    chip = lax.axis_index("x") ^ (offset ^ (2 * (offset % 2) * lax.axis_index("c")))
    above = 4 * chip + 2 * lax.axis_index("c") - 1
    sides = (
        (own_ref, carry_ref, decay_of(codes_ref[...])),
        (other_ref, carry_other_ref, other_ref[DECAY_AT : DECAY_AT + 1]),
    )
    for row in range(4):
        inside = jnp.logical_and(above + row >= 0, above + row < ROWS)
        at = jnp.clip(above + row, 0, ROWS - 1)
        for side, (ref, carried, decay) in enumerate(sides):
            half = pl.ds(pl.multiple_of(at % 2 * COLS, COLS), COLS)
            carry = jnp.where(inside, carried[at // 2, half], 0.0)
            for j in range(FRAMES):
                carry = decay * carry
                state = ref[pl.ds(pl.multiple_of(at * COLS + j * PIX, COLS), COLS)]
                state = jnp.where(inside, state, 0.0) + carry
                spad[j, row, :, side * PD : (side + 1) * PD] = state.astype(BF16)
    rows = [spad[:, di : di + 2].reshape(FRAMES * 2 * COLS, 2 * PD) for di in range(3)]
    taps = []
    for dj in range(3):
        total = jnp.dot(rows[0], w_ref[0, dj], preferred_element_type=F32)
        for di in range(1, 3):
            total = total + jnp.dot(rows[di], w_ref[di, dj], preferred_element_type=F32)
        taps.append(total)
    return shifted_sum(*taps)


def far_kernel(offset, own_ref, other_ref, codes_ref, carry_ref, carry_other_ref, w_ref, after_ref, out_ref, spad):
    out_ref[...] = readout(offset, own_ref, other_ref, codes_ref, carry_ref, carry_other_ref, w_ref, spad)


def join_kernel(piece_ref, relayed_ref, after_ref, out_ref):
    out_ref[...] = piece_ref[...] + relayed_ref[...]


def near_kernel(own_ref, other_ref, codes_ref, carry_ref, carry_other_ref, w_ref, after_ref, x_hbm, gain_ref,
                out_ref, spad, frames, sem):
    start = 4 * lax.axis_index("x") + 2 * lax.axis_index("c")
    copy = pltpu.make_async_copy(x_hbm.at[:, pl.ds(start, 2)], frames, sem)
    copy.start()
    value = readout(0, own_ref, other_ref, codes_ref, carry_ref, carry_other_ref, w_ref, spad)
    copy.wait()
    out_ref[...] = value + frames[...].reshape(FRAMES * 2 * COLS, CIN).astype(F32) * gain_ref[...]


def call(kernel, out, args, spaces=None, scratch=(), flops=0, moved=1 << 20, limit=24, outs=None):
    return pl.pallas_call(
        kernel,
        out_shape=out,
        in_specs=[pl.BlockSpec(memory_space=space) for space in spaces or [pltpu.VMEM] * len(args)],
        out_specs=outs or jax.tree.map(lambda _: pl.BlockSpec(memory_space=pltpu.VMEM), out),
        scratch_shapes=list(scratch),
        compiler_params=pltpu.CompilerParams(vmem_limit_bytes=limit << 20),
        cost_estimate=pl.CostEstimate(flops=flops, bytes_accessed=moved, transcendentals=0),
    )(*args)


def swaps(offset):
    return [(2 * x + c, 2 * (x ^ offset ^ (2 * (offset % 2) * c)) + c) for x in range(4) for c in range(2)]


def shape(*dims, dtype=F32):
    return jax.ShapeDtypeStruct(dims, dtype)


def per_device(frames, in_weight, decay_codes, out_weight, skip_gain):
    codes = decay_codes.reshape(1, PD)
    flops = 2 * FRAMES * PIX * 9 * CIN * PD
    slices = shape(8, PIX // 8, PD)
    owned = FRAMES * 2 * COLS
    shared, end = call(
        drive_kernel,
        (shape(SHARED, PD), slices),
        (frames, in_weight, codes, out_weight),
        spaces=[pltpu.HBM] * 4,
        scratch=(
            pltpu.VMEM((FRAMES, ROWS + 2, COLS, CIN), BF16),
            pltpu.VMEM((3, CIN, 3 * PD), BF16),
            pltpu.VMEM((3, 3, PD, CIN), BF16),
            pltpu.VMEM((1, PD), jnp.int32),
            pltpu.VMEM((SHARED, PD), F32),
            pltpu.SemaphoreType.DMA((FRAMES,)),
            pltpu.SemaphoreType.DMA((9,)),
            pltpu.SemaphoreType.DMA((2,)),
            pltpu.SemaphoreType.DMA((17,)),
        ),
        flops=flops,
        moved=3 << 20,
        limit=59,
        outs=tuple(pl.BlockSpec(memory_space=space) for space in (pltpu.HBM, pltpu.HBM)),
    )
    swap = [(0, 1), (1, 0)]
    ends = lax.all_to_all(end, "z", 0, 0, tiled=True)
    other = lax.ppermute(shared, "c", swap)
    total = call(total_kernel, slices, (ends, codes))
    totals = lax.all_to_all(total, "y", 0, 0, tiled=True)
    carries, weights = call(
        carry_kernel,
        (slices, shape(3, 3, 2 * PD, CIN, dtype=BF16)),
        (ends, totals, codes, out_weight, other),
    )
    carry = lax.all_to_all(carries, "z", 0, 0, tiled=True)
    carry_other = lax.ppermute(carry, "c", swap)
    inputs = (shared, other, codes, carry, carry_other, weights)
    padded = pltpu.VMEM((FRAMES, 4, COLS, 2 * PD), BF16)

    def far(offset, after):
        return call(
            functools.partial(far_kernel, offset),
            shape(owned, CIN),
            (*inputs, after),
            spaces=[pltpu.VMEM] * 6 + [pl.ANY],
            scratch=(padded,),
            flops=flops // 4,
        )

    def send(piece, to):
        return lax.ppermute(piece, ("x", "c"), swaps(to))

    opposite = far(OPPOSITE, carry_other)
    relayed = send(opposite, FIRST)
    piece = far(FIRST, opposite)
    first = send(piece, FIRST)
    piece = far(LAST, piece)
    own = call(
        near_kernel,
        shape(owned, CIN),
        (*inputs, piece, frames, skip_gain.reshape(1, CIN)),
        spaces=[pltpu.VMEM] * 6 + [pl.ANY, pltpu.HBM, pltpu.VMEM],
        scratch=(padded, pltpu.VMEM((FRAMES, 2, COLS, CIN), BF16), pltpu.SemaphoreType.DMA),
        flops=flops // 4,
    )
    piece = call(
        join_kernel, shape(owned, CIN), (piece, relayed, own), spaces=[pltpu.VMEM] * 2 + [pl.ANY]
    )
    last = send(piece, LAST)
    ready = call(
        join_kernel, shape(owned, CIN), (own, first, piece), spaces=[pltpu.VMEM] * 2 + [pl.ANY]
    )
    mixed = call(mix_kernel, shape(owned, CIN, dtype=BF16), (ready, last))
    return mixed.reshape(FRAMES, 2, COLS, CIN)


def solution(mesh):
    finer = Mesh(mesh.devices.reshape(8, 8, 4, 2), ("y", "z", "x", "c"))
    chan = ("x", "c")
    placed = (
        P(("y", "z"), None, None, None),
        P(None, None, None, chan),
        P(chan),
        P(None, None, chan, None),
        P(),
    )
    return jax.shard_map(
        per_device,
        mesh=finer,
        in_specs=placed,
        out_specs=P(("y", "z"), chan, None, None),
        check_vma=False,
    )
```

```python
import functools


import jax
import jax.numpy as jnp
from jax import lax
from jax.experimental import pallas as pl
from jax.experimental.pallas import tpu as pltpu
from jax.sharding import Mesh
from jax.sharding import PartitionSpec as P

FRAMES, ROWS, COLS, CIN, PD = 8, 16, 16, 256, 128
PIX = ROWS * COLS
DECAY_AT = FRAMES * PIX
WEIGHT_AT = DECAY_AT + 8
SHARED = WEIGHT_AT + 18 * PD
OPPOSITE, FIRST, LAST = 2, 1, 3
F32, BF16 = jnp.float32, jnp.bfloat16


def decay_of(codes):
    return 1.0 - codes.astype(F32) / 4096.0


def pow8(value):
    value = value * value
    value = value * value
    return value * value


def shifted_sum(left, centre, right):
    count = left.shape[0]
    column = lax.broadcasted_iota(jnp.int32, left.shape, 0) % COLS
    from_left = jnp.where(column == 0, 0.0, pltpu.roll(left, 1, 0))
    from_right = jnp.where(column == COLS - 1, 0.0, pltpu.roll(right, count - 1, 0))
    return from_left + centre + from_right


def drive_kernel(x_hbm, w_hbm, codes_hbm, wout_hbm, shared_hbm, end_hbm,
                 xpad, wcat, wout, codes, shared, frame_sem, tap_sem, small_sem, out_sem):
    taps = [(di, dj) for di in range(3) for dj in range(3)]
    copies = [
        pltpu.make_async_copy(w_hbm.at[di, dj], wcat.at[di, :, pl.ds(dj * PD, PD)], tap_sem.at[3 * di + dj])
        for di, dj in taps
    ]
    frames = [
        pltpu.make_async_copy(x_hbm.at[j], xpad.at[j, pl.ds(1, ROWS)], frame_sem.at[j]) for j in range(FRAMES)
    ]
    small = [
        pltpu.make_async_copy(src, dst, small_sem.at[i])
        for i, (src, dst) in enumerate(((codes_hbm, codes), (wout_hbm, wout)))
    ]
    group = FRAMES // 2
    edges = [*range(0, DECAY_AT, PIX), DECAY_AT, SHARED]
    sends = [
        pltpu.make_async_copy(shared.at[pl.ds(at, to - at)], shared_hbm.at[pl.ds(at, to - at)], out_sem.at[i])
        for i, (at, to) in enumerate(zip(edges[:-1], edges[1:], strict=True))
    ]
    last, part = DECAY_AT - PIX, PIX // 8
    ends = [
        pltpu.make_async_copy(shared.at[pl.ds(last + i * part, part)], end_hbm.at[i], out_sem.at[len(sends) + i])
        for i in range(8)
    ]
    for copy in [small[0], *copies[:3], *frames[:group], *copies[3:], *frames[group:], small[1]]:
        copy.start()
    xpad[:, 0] = jnp.zeros((FRAMES, COLS, CIN), BF16)
    xpad[:, ROWS + 1] = jnp.zeros((FRAMES, COLS, CIN), BF16)
    small[0].wait()
    decay = decay_of(codes[...])
    shared[DECAY_AT:WEIGHT_AT] = jnp.broadcast_to(decay, (8, PD))
    running = jnp.zeros((PIX, PD), F32)
    for first in range(0, FRAMES, group):
        for copy in frames[first : first + group]:
            copy.wait()
        total = jnp.zeros((group * PIX, 3 * PD), F32)
        for di in range(3):
            if first == 0:
                for copy in copies[3 * di : 3 * di + 3]:
                    copy.wait()
            rows = xpad[first : first + group, di : di + ROWS].reshape(group * PIX, CIN)
            total = total + jnp.dot(rows, wcat[di], preferred_element_type=F32)
        drive = shifted_sum(total[:, :PD], total[:, PD : 2 * PD], total[:, 2 * PD :])
        for k in range(group):
            frame = first + k
            running = decay * running + drive[k * PIX : (k + 1) * PIX]
            shared[frame * PIX : (frame + 1) * PIX] = running
            if frame < FRAMES - 1:
                sends[frame].start()
        if first == 0:
            small[1].wait()
            for tap in range(9):
                for half in range(2):
                    at = WEIGHT_AT + (2 * tap + half) * PD
                    shared[at : at + PD] = wout[tap // 3, tap % 3, :, half * PD : (half + 1) * PD].astype(F32)
            sends[-1].start()
    for copy in ends:
        copy.start()
    sends[FRAMES - 1].start()
    for copy in ends + sends:
        copy.wait()


def total_kernel(ends_ref, codes_ref, out_ref):
    a8 = pow8(decay_of(codes_ref[...]))
    total = ends_ref[0]
    for z in range(1, 8):
        total = a8 * total + ends_ref[z]
    for y in range(8):
        out_ref[y] = total


def mix_kernel(own_ref, first_ref, last_ref, out_ref):
    value = own_ref[...] + first_ref[...] + last_ref[...]
    half = 0.5 * value
    mixed = half + half * lax.erf(value * (0.5**0.5))
    out_ref[...] = mixed.astype(BF16)


def carry_kernel(ends_ref, totals_ref, codes_ref, wout_ref, other_ref, out_ref, w_ref):
    a8 = pow8(decay_of(codes_ref[...]))
    a64 = pow8(a8)
    own = lax.axis_index("y")
    carry = jnp.zeros((PIX // 8, PD), F32)
    for y in range(8):
        carry = jnp.where(y < own, a64 * carry + totals_ref[y], carry)
    for z in range(8):
        out_ref[z] = carry
        carry = a8 * carry + ends_ref[z]
    w_ref[:, :, :PD] = wout_ref[...]
    for tap in range(9):
        for half in range(2):
            at = WEIGHT_AT + (2 * tap + half) * PD
            w_ref[tap // 3, tap % 3, PD:, half * PD : (half + 1) * PD] = other_ref[at : at + PD].astype(BF16)


def readout(offset, own_ref, other_ref, codes_ref, carry_ref, carry_other_ref, w_ref, spad):
    chip = lax.axis_index("x") ^ (offset ^ (2 * (offset % 2) * lax.axis_index("c")))
    above = 4 * chip + 2 * lax.axis_index("c") - 1
    sides = (
        (own_ref, carry_ref, decay_of(codes_ref[...])),
        (other_ref, carry_other_ref, other_ref[DECAY_AT : DECAY_AT + 1]),
    )
    for row in range(4):
        inside = jnp.logical_and(above + row >= 0, above + row < ROWS)
        at = jnp.clip(above + row, 0, ROWS - 1)
        for side, (ref, carried, decay) in enumerate(sides):
            half = pl.ds(pl.multiple_of(at % 2 * COLS, COLS), COLS)
            carry = jnp.where(inside, carried[at // 2, half], 0.0)
            for j in range(FRAMES):
                carry = decay * carry
                state = ref[pl.ds(pl.multiple_of(at * COLS + j * PIX, COLS), COLS)]
                state = jnp.where(inside, state, 0.0) + carry
                spad[j, row, :, side * PD : (side + 1) * PD] = state.astype(BF16)
    rows = [spad[:, di : di + 2].reshape(FRAMES * 2 * COLS, 2 * PD) for di in range(3)]
    taps = []
    for dj in range(3):
        total = jnp.dot(rows[0], w_ref[0, dj], preferred_element_type=F32)
        for di in range(1, 3):
            total = total + jnp.dot(rows[di], w_ref[di, dj], preferred_element_type=F32)
        taps.append(total)
    return shifted_sum(*taps)


def far_kernel(offset, own_ref, other_ref, codes_ref, carry_ref, carry_other_ref, w_ref, after_ref, out_ref, spad):
    out_ref[...] = readout(offset, own_ref, other_ref, codes_ref, carry_ref, carry_other_ref, w_ref, spad)


def join_kernel(piece_ref, relayed_ref, after_ref, out_ref):
    out_ref[...] = piece_ref[...] + relayed_ref[...]


def near_kernel(own_ref, other_ref, codes_ref, carry_ref, carry_other_ref, w_ref, after_ref, x_hbm, gain_ref,
                out_ref, spad, frames, sem):
    start = 4 * lax.axis_index("x") + 2 * lax.axis_index("c")
    copy = pltpu.make_async_copy(x_hbm.at[:, pl.ds(start, 2)], frames, sem)
    copy.start()
    value = readout(0, own_ref, other_ref, codes_ref, carry_ref, carry_other_ref, w_ref, spad)
    copy.wait()
    out_ref[...] = value + frames[...].reshape(FRAMES * 2 * COLS, CIN).astype(F32) * gain_ref[...]


def call(kernel, out, args, spaces=None, scratch=(), flops=0, moved=1 << 20, limit=24, outs=None):
    return pl.pallas_call(
        kernel,
        out_shape=out,
        in_specs=[pl.BlockSpec(memory_space=space) for space in spaces or [pltpu.VMEM] * len(args)],
        out_specs=outs or jax.tree.map(lambda _: pl.BlockSpec(memory_space=pltpu.VMEM), out),
        scratch_shapes=list(scratch),
        compiler_params=pltpu.CompilerParams(vmem_limit_bytes=limit << 20),
        cost_estimate=pl.CostEstimate(flops=flops, bytes_accessed=moved, transcendentals=0),
    )(*args)


def swaps(offset):
    return [(2 * x + c, 2 * (x ^ offset ^ (2 * (offset % 2) * c)) + c) for x in range(4) for c in range(2)]


def shape(*dims, dtype=F32):
    return jax.ShapeDtypeStruct(dims, dtype)


def per_device(frames, in_weight, decay_codes, out_weight, skip_gain):
    codes = decay_codes.reshape(1, PD)
    flops = 2 * FRAMES * PIX * 9 * CIN * PD
    slices = shape(8, PIX // 8, PD)
    owned = FRAMES * 2 * COLS
    shared, end = call(
        drive_kernel,
        (shape(SHARED, PD), slices),
        (frames, in_weight, codes, out_weight),
        spaces=[pltpu.HBM] * 4,
        scratch=(
            pltpu.VMEM((FRAMES, ROWS + 2, COLS, CIN), BF16),
            pltpu.VMEM((3, CIN, 3 * PD), BF16),
            pltpu.VMEM((3, 3, PD, CIN), BF16),
            pltpu.VMEM((1, PD), jnp.int32),
            pltpu.VMEM((SHARED, PD), F32),
            pltpu.SemaphoreType.DMA((FRAMES,)),
            pltpu.SemaphoreType.DMA((9,)),
            pltpu.SemaphoreType.DMA((2,)),
            pltpu.SemaphoreType.DMA((17,)),
        ),
        flops=flops,
        moved=3 << 20,
        limit=59,
        outs=tuple(pl.BlockSpec(memory_space=space) for space in (pltpu.HBM, pltpu.HBM)),
    )
    swap = [(0, 1), (1, 0)]
    ends = lax.all_to_all(end, "z", 0, 0, tiled=True)
    other = lax.ppermute(shared, "c", swap)
    total = call(total_kernel, slices, (ends, codes))
    totals = lax.all_to_all(total, "y", 0, 0, tiled=True)
    carries, weights = call(
        carry_kernel,
        (slices, shape(3, 3, 2 * PD, CIN, dtype=BF16)),
        (ends, totals, codes, out_weight, other),
    )
    carry = lax.all_to_all(carries, "z", 0, 0, tiled=True)
    carry_other = lax.ppermute(carry, "c", swap)
    inputs = (shared, other, codes, carry, carry_other, weights)
    padded = pltpu.VMEM((FRAMES, 4, COLS, 2 * PD), BF16)

    def far(offset, after):
        return call(
            functools.partial(far_kernel, offset),
            shape(owned, CIN),
            (*inputs, after),
            spaces=[pltpu.VMEM] * 6 + [pl.ANY],
            scratch=(padded,),
            flops=flops // 4,
        )

    def send(piece, to):
        return lax.ppermute(piece, ("x", "c"), swaps(to))

    opposite = far(OPPOSITE, carry_other)
    relayed = send(opposite, FIRST)
    piece = far(FIRST, opposite)
    first = send(piece, FIRST)
    piece = far(LAST, piece)
    piece = call(
        join_kernel, shape(owned, CIN), (piece, relayed, piece), spaces=[pltpu.VMEM] * 2 + [pl.ANY]
    )
    last = send(piece, LAST)
    own = call(
        near_kernel,
        shape(owned, CIN),
        (*inputs, piece, frames, skip_gain.reshape(1, CIN)),
        spaces=[pltpu.VMEM] * 6 + [pl.ANY, pltpu.HBM, pltpu.VMEM],
        scratch=(padded, pltpu.VMEM((FRAMES, 2, COLS, CIN), BF16), pltpu.SemaphoreType.DMA),
        flops=flops // 4,
    )
    mixed = call(mix_kernel, shape(owned, CIN, dtype=BF16), (own, first, last))
    return mixed.reshape(FRAMES, 2, COLS, CIN)


def solution(mesh):
    finer = Mesh(mesh.devices.reshape(8, 8, 4, 2), ("y", "z", "x", "c"))
    chan = ("x", "c")
    placed = (
        P(("y", "z"), None, None, None),
        P(None, None, None, chan),
        P(chan),
        P(None, None, chan, None),
        P(),
    )
    return jax.shard_map(
        per_device,
        mesh=finer,
        in_specs=placed,
        out_specs=P(("y", "z"), chan, None, None),
        check_vma=False,
    )
```
